512 devices in a mesh: grp: 8 (over y, z_hi), blk: 64 (over x, z_lo, core).
Axes of the slice: x: 4, y: 4, z: 16 (z_hi: 2, z_lo: 8; z = z_hi * 8 + z_lo), core: 2. Of those that a mesh axis runs over, the one named last changes fastest.
Arguments:
- images: bfloat16 [16384, 1152], P(('blk', 'grp')), may hold values from -6 to 6
- texts: bfloat16 [16384, 1152], P(('blk', 'grp')), may hold values from -6 to 6
- tile_mask: int32 [128, 128], replicated, may hold values from 0 to 1, as said below
Outputs:
- image_grads: float32 [16384, 1152], P(('blk', 'grp'))
- text_grads: float32 [16384, 1152], P(('blk', 'grp'))
- loss_mean: float32 [], replicated
The draws below stay inside these ranges and needn't reach their ends.
Inputs may be any that keep to these rules, and one draw needn't show every extreme that they name: tile_mask is symmetric and 1 on its diagonal.
All inputs are finite; a program needn't handle non-finite values.
Results may differ from the reference program's by a relative error of at most 0.00045.
The reference program's roundings to bfloat16 on the way (of `coef`) count: a program that leaves them out, or rounds other values in their place, can miss the bound.
Values may be sent and summed in bfloat16 or wider, within the bound.
No kernel may reach another device: no remote copies, remote signals or barrier semaphores. Data moves between devices by JAX's collectives and lax.ppermute only.
A program may use at most 64 MiB of HBM per device.

```python
import math
import jax
import jax.numpy as jnp
from jax import lax

E = 1152
TILE = 128
TOTAL = 16384
TILES = 128


def draw_tile_mask(key, part):
    rows = jnp.arange(TILES, dtype=jnp.int32)[:, None]
    cols = jnp.arange(TILES, dtype=jnp.int32)[None, :]
    level = jax.random.randint(key, (TILES, TILES), 0, 4 * TILES)
    upper = (level >= rows + cols + TILES // 4).astype(jnp.int32)
    lower_index = jnp.minimum(rows, cols)
    upper_index = jnp.maximum(rows, cols)
    mirrored = upper[lower_index, upper_index]
    return jnp.where(rows == cols, 1, mirrored).astype(jnp.int32)


def shard_levels(own_key, extent, pieces, least, high):
    gain, own = 1.0, jax.random.fold_in(own_key, 6)
    for dim, parts in pieces:
        draws = jnp.exp(jax.random.uniform(jax.random.fold_in(own, dim), (parts,), jnp.float32, least / len(pieces), high / len(pieces)))
        gain = gain * jnp.repeat(draws, extent[dim] // parts).reshape([-1 if axis == dim else 1 for axis in range(len(extent))])
    return gain


def normal_values(key, dims, scale, reach, cuts=(), held_as=jnp.bfloat16):
    values = jax.random.normal(key, dims, jnp.float32) * scale
    if len(cuts) > 0:
        values = shard_levels(key, dims, cuts, -0.22, 0.18) * values
    return jnp.clip(values, min=-reach, max=reach).astype(held_as)


def setup_inputs(seed: int = 0) -> dict:
    keys = jax.random.split(jax.random.key(seed), 4)
    images = normal_values(keys[0], (TOTAL, E), 1.0, 6.0, ((0, 512),))
    texts = normal_values(keys[1], (TOTAL, E), 1.0, 6.0, ((0, 512),))
    tile_mask = draw_tile_mask(jax.random.fold_in(keys[3], 71), 0)
    return dict(images=images, texts=texts, tile_mask=tile_mask)


TEMP = 10.0
BIAS = -2.0
EPS = 1e-06

def normalize(values):
    return values * lax.rsqrt(lax.optimization_barrier(jnp.sum(values * values, axis=-1, keepdims=True)) + EPS)

def reference(images, texts, tile_mask):
    image_unit, image_back = jax.vjp(normalize, images.astype(jnp.float32))
    text_unit, text_back = jax.vjp(normalize, texts.astype(jnp.float32))
    image_bf = image_unit.astype(jnp.bfloat16)
    text_bf = text_unit.astype(jnp.bfloat16)
    all_ids = jnp.arange(TOTAL, dtype=jnp.int32)
    tile_ids = jnp.arange(TILES, dtype=jnp.int32)
    text_hot = (tile_ids[:, None] == (all_ids // TILE)[None, :]).astype(jnp.float32)
    mask_values = tile_mask.astype(jnp.float32)
    block = math.gcd(TOTAL, 512)
    starts = jnp.arange(TOTAL // block, dtype=jnp.int32) * block

    def step(carry, start):
        text_sums, loss_sum, pair_count = carry
        ids = start + jnp.arange(block, dtype=jnp.int32)
        hot = ((ids // TILE)[:, None] == tile_ids[None, :]).astype(jnp.float32)
        masked = jnp.dot(jnp.dot(hot, mask_values, precision=lax.Precision.HIGHEST), text_hot, precision=lax.Precision.HIGHEST)
        matched = ids[:, None] == all_ids[None, :]
        valid = (masked < 0.5) | matched
        rows_bf = lax.dynamic_slice_in_dim(image_bf, start, block, 0)
        logits = TEMP * jnp.dot(rows_bf, text_bf.T, preferred_element_type=jnp.float32) + BIAS
        signs = jnp.where(matched, 1.0, -1.0)
        loss_sum = loss_sum + jnp.sum(jnp.where(valid, jax.nn.softplus(-signs * logits), 0.0))
        pair_count = pair_count + jnp.sum(valid.astype(jnp.float32))
        coef = jnp.where(valid, jax.nn.sigmoid(logits) - matched.astype(jnp.float32), 0.0).astype(jnp.bfloat16)
        image_part = TEMP * jnp.dot(coef, text_bf, preferred_element_type=jnp.float32)
        text_sums = text_sums + jnp.dot(coef.T, rows_bf, preferred_element_type=jnp.float32)
        return ((text_sums, loss_sum, pair_count), image_part)
    initial = (jnp.zeros((TOTAL, E), jnp.float32), jnp.zeros((), jnp.float32), jnp.zeros((), jnp.float32))
    (text_sums, loss_sum, pair_count), image_parts = lax.scan(step, initial, starts)
    image_sums = image_parts.reshape(TOTAL, E)
    image_grads = image_back(image_sums)[0]
    text_grads = text_back(TEMP * text_sums)[0]
    return (image_grads, text_grads, loss_sum / pair_count)
```

```python
import jax
import jax.numpy as jnp
from jax import lax
from jax.sharding import Mesh
from jax.sharding import PartitionSpec as P

TILE = 128
TEMP = 10.0
BIAS = -2.0
EPS = 1e-06
ROWS_AXES = ("x", "zb", "za", "c", "y", "zh")
ZB = ("zh", "zb")
SIDE = 4
DIGITS = 6
BASE = 2048.0
SPARE = 16


def spread(block, axis):
    sent = jnp.broadcast_to(block[None], (SIDE, *block.shape))
    return lax.all_to_all(sent, axis, 0, 0, tiled=True)


def swapped(value):
    return lax.ppermute(value, "c", [(0, 1), (1, 0)])


def inverse_norm(values):
    return lax.rsqrt(jnp.sum(values * values, axis=-1, keepdims=True) + EPS)


def to_row(total, width):
    lanes = lax.broadcasted_iota(jnp.int32, (1, width), 1)
    row = jnp.zeros((1, width), jnp.float32)
    rest = total * 2.0**-32
    for k in range(DIGITS):
        rest = rest * BASE
        digit = jnp.floor(rest)
        rest = rest - digit
        row = jnp.where(lanes == k, digit, row)
    return row


def from_rows(rows):
    lanes = lax.broadcasted_iota(jnp.int32, rows.shape, 1)
    worth = jnp.zeros(rows.shape, jnp.float32)
    for k in range(DIGITS):
        worth = jnp.where(lanes == k, 2.0**32 / BASE ** (k + 1), worth)
    return jnp.sum(rows * worth)


def sent_and_summed(parts, total, axis):
    side, rows, width = parts.shape
    spare = jnp.broadcast_to(to_row(total, width)[None], (side, SPARE, width))
    sent = jnp.concatenate([parts.astype(jnp.float16), spare.astype(jnp.float16)], axis=1)
    got = lax.all_to_all(sent, axis, 0, 0, tiled=True)
    sums = jnp.sum(got[:, :rows].astype(jnp.float32), axis=0)
    return sums, from_rows(got[:, rows].astype(jnp.float32))


def block_mask(tile_mask):
    x, zb, za, c, y = (lax.axis_index(n) for n in ("x", "zb", "za", "c", "y"))
    tiles = tile_mask.shape[0]

    def tile_of(xs, zbs, zas, cs, ys):
        return (((xs * 2 + zbs) * 4 + zas) * 2 + cs) * 2 + ys // 2

    k = jnp.arange(16, dtype=jnp.int32)
    image_tiles = tile_of(k // 4, zb, k % 4, c, y)
    k = jnp.arange(32, dtype=jnp.int32)
    text_cores = jnp.where(k < 16, c, 1 - c)
    text_tiles = tile_of(x, k % 2, za, text_cores, (k // 4) % 4)
    every = jnp.arange(tiles, dtype=jnp.int32)
    left = (image_tiles[:, None] == every[None]).astype(jnp.float32)
    right = (every[:, None] == text_tiles[None]).astype(jnp.float32)
    return jnp.dot(jnp.dot(left, tile_mask.astype(jnp.float32)), right)


def pair_codes(tile_mask, rows):
    x, za, y, zb = (lax.axis_index(n) for n in ("x", "za", "y", ZB))
    own_image = x * 4 + za
    own_text = y * 4 + zb
    masked = block_mask(tile_mask)
    i = jnp.arange(16 * rows, dtype=jnp.int32)
    j = jnp.arange(32 * rows, dtype=jnp.int32)
    left = (i[:, None] // rows == jnp.arange(16)[None]).astype(jnp.float32)
    right = (jnp.arange(32)[:, None] == j[None] // rows).astype(jnp.float32)
    masked = jnp.dot(jnp.dot(left, masked), right)
    matched = (i - own_image * rows)[:, None] == (j - own_text * rows)[None]
    matched = matched & (i // rows == own_image)[:, None]
    return jnp.where(matched, 2.0, jnp.where(masked < 0.5, 1.0, 0.0)).astype(jnp.bfloat16)


def back(values, inverse, grads):
    unit = values * inverse
    return inverse * (grads - unit * jnp.sum(unit * grads, axis=-1, keepdims=True))


def on_device(images, texts, tile_mask):
    rows, width = images.shape
    images = images.astype(jnp.float32)
    texts = texts.astype(jnp.float32)
    text_inverse = inverse_norm(texts)
    image_inverse = inverse_norm(images)
    text_bf = (texts * text_inverse).astype(jnp.bfloat16)
    image_bf = (images * image_inverse).astype(jnp.bfloat16)

    own_texts = spread(text_bf, ZB).reshape(SIDE * rows, width)
    own_texts = spread(own_texts, "y").reshape(16 * rows, width)
    other_texts = swapped(own_texts)
    near = spread(image_bf, "za").reshape(SIDE * rows, width)
    group = spread(near, "x").reshape(16 * rows, width)
    group_texts = jnp.concatenate([own_texts, other_texts], axis=0)

    codes = pair_codes(tile_mask, rows)
    valid = codes > 0.5
    matched = codes > 1.5
    logits = (
        TEMP
        * lax.dot_general(
            group, group_texts, (((1,), (1,)), ((), ())), preferred_element_type=jnp.float32
        )
        + BIAS
    )
    signs = jnp.where(matched, 1.0, -1.0)
    loss = jnp.sum(jnp.where(valid, jax.nn.softplus(-signs * logits), 0.0))
    coef = jnp.where(valid, jax.nn.sigmoid(logits) - matched.astype(jnp.float32), 0.0).astype(
        jnp.bfloat16
    )
    loss = loss + swapped(loss)
    image_parts = jnp.dot(coef, group_texts, preferred_element_type=jnp.float32)
    text_parts = lax.dot_general(
        coef, group, (((0,), (0,)), ((), ())), preferred_element_type=jnp.float32
    )
    text_parts = text_parts[: 16 * rows] + swapped(text_parts[16 * rows :])

    image_parts, loss = sent_and_summed(image_parts.reshape(SIDE, SIDE * rows, width), loss, "x")
    image_sums, loss = sent_and_summed(image_parts.reshape(SIDE, rows, width), loss, "za")
    text_parts, loss = sent_and_summed(text_parts.reshape(SIDE, SIDE * rows, width), loss, "y")
    text_sums, loss = sent_and_summed(text_parts.reshape(SIDE, rows, width), loss, ZB)

    zero = tile_mask == 0
    size = tile_mask.shape[0]
    diagonal = jnp.eye(size, dtype=jnp.bool_)
    pairs = jnp.sum(jnp.where(zero, TILE * TILE, jnp.where(diagonal, TILE, 0)))
    return (
        back(images, image_inverse, TEMP * image_sums),
        back(texts, text_inverse, TEMP * text_sums),
        loss / pairs.astype(jnp.float32),
    )


def solution(mesh):
    finer = Mesh(mesh.devices.reshape(4, 2, 4, 2, 4, 2), ("y", "zh", "x", "zb", "za", "c"))
    placed = P(ROWS_AXES, None)
    return jax.shard_map(
        on_device,
        mesh=finer,
        in_specs=(placed, placed, P()),
        out_specs=(placed, placed, P()),
        check_vma=False,
    )
```

```python
import jax
import jax.numpy as jnp
from jax import lax
from jax.sharding import Mesh
from jax.sharding import PartitionSpec as P

TILE = 128
TEMP = 10.0
BIAS = -2.0
EPS = 1e-06
ROWS_AXES = ("x", "zb", "za", "c", "y", "zh")
ZB = ("zh", "zb")
SIDE = 4
DIGITS = 6
BASE = 2048.0
SPARE = 16


def spread(block, axis):
    sent = jnp.broadcast_to(block[None], (SIDE, *block.shape))
    return lax.all_to_all(sent, axis, 0, 0, tiled=True)


def swapped(value):
    return lax.ppermute(value, "c", [(0, 1), (1, 0)])


def turned(value, axis, steps):
    return lax.ppermute(value, axis, [(k, (k + steps) % SIDE) for k in range(SIDE)])


def spread_turning(block, axis):
    return jnp.concatenate([block] + [turned(block, axis, k) for k in range(1, SIDE)], axis=0)


def turned_and_summed(parts, axis):
    sums = parts[0]
    got = [turned(parts[k].astype(jnp.float16), axis, -k) for k in range(1, SIDE)]
    for part in got:
        sums = sums + part.astype(jnp.float32)
    return sums


def over_image_group(total):
    axes = ("x", "za", "c")
    count = lax.axis_size(axes)
    sent = jnp.broadcast_to(total, (count, 8, 128))
    return jnp.sum(lax.all_to_all(sent, axes, 0, 0, tiled=True)[:, 0, 0])


def inverse_norm(values):
    return lax.rsqrt(jnp.sum(values * values, axis=-1, keepdims=True) + EPS)


def to_row(total, width):
    lanes = lax.broadcasted_iota(jnp.int32, (1, width), 1)
    row = jnp.zeros((1, width), jnp.float32)
    rest = total * 2.0**-32
    for k in range(DIGITS):
        rest = rest * BASE
        digit = jnp.floor(rest)
        rest = rest - digit
        row = jnp.where(lanes == k, digit, row)
    return row


def from_rows(rows):
    lanes = lax.broadcasted_iota(jnp.int32, rows.shape, 1)
    worth = jnp.zeros(rows.shape, jnp.float32)
    for k in range(DIGITS):
        worth = jnp.where(lanes == k, 2.0**32 / BASE ** (k + 1), worth)
    return jnp.sum(rows * worth)


def sent_and_summed(parts, total, axis):
    side, rows, width = parts.shape
    spare = jnp.broadcast_to(to_row(total, width)[None], (side, SPARE, width))
    sent = jnp.concatenate([parts.astype(jnp.float16), spare.astype(jnp.float16)], axis=1)
    got = lax.all_to_all(sent, axis, 0, 0, tiled=True)
    sums = jnp.sum(got[:, :rows].astype(jnp.float32), axis=0)
    return sums, from_rows(got[:, rows].astype(jnp.float32))


def block_mask(tile_mask):
    x, zb, za, c, y = (lax.axis_index(n) for n in ("x", "zb", "za", "c", "y"))
    tiles = tile_mask.shape[0]

    def tile_of(xs, zbs, zas, cs, ys):
        return (((xs * 2 + zbs) * 4 + zas) * 2 + cs) * 2 + ys // 2

    k = jnp.arange(16, dtype=jnp.int32)
    image_tiles = tile_of((x - k // 4) % 4, zb, (za - k % 4) % 4, c, y)
    k = jnp.arange(32, dtype=jnp.int32)
    text_cores = jnp.where(k < 16, c, 1 - c)
    text_tiles = tile_of(x, k % 2, za, text_cores, (k // 4) % 4)
    every = jnp.arange(tiles, dtype=jnp.int32)
    left = (image_tiles[:, None] == every[None]).astype(jnp.float32)
    right = (every[:, None] == text_tiles[None]).astype(jnp.float32)
    return jnp.dot(jnp.dot(left, tile_mask.astype(jnp.float32)), right)


def pair_codes(tile_mask, rows):
    own_text = lax.axis_index("y") * 4 + lax.axis_index(ZB)
    masked = block_mask(tile_mask)
    i = jnp.arange(16 * rows, dtype=jnp.int32)
    j = jnp.arange(32 * rows, dtype=jnp.int32)
    left = (i[:, None] // rows == jnp.arange(16)[None]).astype(jnp.float32)
    right = (jnp.arange(32)[:, None] == j[None] // rows).astype(jnp.float32)
    masked = jnp.dot(jnp.dot(left, masked), right)
    matched = i[:, None] == (j - own_text * rows)[None]
    matched = matched & (i < rows)[:, None]
    return jnp.where(matched, 2.0, jnp.where(masked < 0.5, 1.0, 0.0)).astype(jnp.bfloat16)


def back(values, inverse, grads):
    unit = values * inverse
    return inverse * (grads - unit * jnp.sum(unit * grads, axis=-1, keepdims=True))


def on_device(images, texts, tile_mask):
    rows, width = images.shape
    images = images.astype(jnp.float32)
    texts = texts.astype(jnp.float32)
    text_inverse = inverse_norm(texts)
    image_inverse = inverse_norm(images)
    text_bf = (texts * text_inverse).astype(jnp.bfloat16)
    image_bf = (images * image_inverse).astype(jnp.bfloat16)

    own_texts = spread(text_bf, ZB).reshape(SIDE * rows, width)
    own_texts = spread(own_texts, "y").reshape(16 * rows, width)
    other_texts = swapped(own_texts)
    group = spread_turning(spread_turning(image_bf, "za"), "x")
    group_texts = jnp.concatenate([own_texts, other_texts], axis=0)

    codes = pair_codes(tile_mask, rows)
    valid = codes > 0.5
    matched = codes > 1.5
    logits = (
        TEMP
        * lax.dot_general(
            group, group_texts, (((1,), (1,)), ((), ())), preferred_element_type=jnp.float32
        )
        + BIAS
    )
    signs = jnp.where(matched, 1.0, -1.0)
    loss = jnp.sum(jnp.where(valid, jax.nn.softplus(-signs * logits), 0.0))
    coef = jnp.where(valid, jax.nn.sigmoid(logits) - matched.astype(jnp.float32), 0.0).astype(
        jnp.bfloat16
    )
    loss = over_image_group(loss)
    image_parts = jnp.dot(coef, group_texts, preferred_element_type=jnp.float32)
    text_parts = lax.dot_general(
        coef, group, (((0,), (0,)), ((), ())), preferred_element_type=jnp.float32
    )
    text_parts = text_parts[: 16 * rows] + swapped(text_parts[16 * rows :])

    image_parts = turned_and_summed(image_parts.reshape(SIDE, SIDE * rows, width), "x")
    image_sums = turned_and_summed(image_parts.reshape(SIDE, rows, width), "za")
    text_parts, loss = sent_and_summed(text_parts.reshape(SIDE, SIDE * rows, width), loss, "y")
    text_sums, loss = sent_and_summed(text_parts.reshape(SIDE, rows, width), loss, ZB)

    zero = tile_mask == 0
    size = tile_mask.shape[0]
    diagonal = jnp.eye(size, dtype=jnp.bool_)
    pairs = jnp.sum(jnp.where(zero, TILE * TILE, jnp.where(diagonal, TILE, 0)))
    return (
        back(images, image_inverse, TEMP * image_sums),
        back(texts, text_inverse, TEMP * text_sums),
        loss / pairs.astype(jnp.float32),
    )


def solution(mesh):
    finer = Mesh(mesh.devices.reshape(4, 2, 4, 2, 4, 2), ("y", "zh", "x", "zb", "za", "c"))
    placed = P(ROWS_AXES, None)
    return jax.shard_map(
        on_device,
        mesh=finer,
        in_specs=(placed, placed, P()),
        out_specs=(placed, placed, P()),
        check_vma=False,
    )
```

```python
import jax
import jax.numpy as jnp
from jax import lax
from jax.experimental import pallas as pl
from jax.experimental.pallas import tpu as pltpu
from jax.sharding import Mesh
from jax.sharding import PartitionSpec as P


TILE = 128
TEMP = 10.0
BIAS = -2.0
EPS = 1e-06
ROWS_AXES = ("x", "zb", "za", "c", "y", "zh")
ZB = ("zh", "zb")
SIDE = 4
DIGITS = 7
BASE = 512.0
TOP = 2.0**32
SPARE = 128
CHUNK = 256

VMEM = pl.BlockSpec(memory_space=pltpu.VMEM)


def inverse_norm(values):
    return lax.rsqrt(jnp.sum(values * values, axis=-1, keepdims=True) + EPS)


def slots_kernel(values_ref, slots_ref):
    values = values_ref[...].astype(jnp.float32)
    unit = (values * inverse_norm(values)).astype(jnp.bfloat16)
    for k in range(SIDE):
        slots_ref[k] = unit


def normalized_slots(values):
    return pl.pallas_call(
        slots_kernel,
        out_shape=pltpu.VMEM((SIDE, *values.shape), jnp.bfloat16),
        in_specs=[VMEM],
        out_specs=VMEM,
        compiler_params=pltpu.CompilerParams(vmem_limit_bytes=4 * 2**20),
    )(values)


def pair_kernel(codes_ref, *refs):
    part_refs, (own_ref, other_ref) = refs[:SIDE], refs[SIDE : SIDE + 2]
    coef_ref, own_sums_ref, other_sums_ref, loss_ref, group_ref = refs[SIDE + 2 :]
    near = part_refs[0].shape[0]
    for k in range(SIDE):
        group_ref[k * near : (k + 1) * near] = part_refs[k][...]
    group = group_ref[...]
    width = group.shape[1]
    half = own_ref.shape[0]
    loss = jnp.zeros((8, group.shape[0]), jnp.float32)
    for texts_ref, sums_ref, base in ((other_ref, other_sums_ref, half), (own_ref, own_sums_ref, 0)):
        for at in range(0, half, CHUNK):
            logits = TEMP * lax.dot_general(
                texts_ref[at : at + CHUNK],
                group,
                (((1,), (1,)), ((), ())),
                preferred_element_type=jnp.float32,
            )
            logits = logits + BIAS
            codes = codes_ref[base + at : base + at + CHUNK].astype(jnp.float32)
            small = jnp.exp(-jnp.abs(logits))
            soft = jnp.maximum(logits, 0.0) + jnp.log1p(small)
            sigmoid = jnp.where(logits >= 0.0, 1.0, small) / (1.0 + small)
            matched = codes > 1.5
            terms = jnp.where(codes > 0.5, soft - jnp.where(matched, logits, 0.0), 0.0)
            loss = loss + jnp.sum(terms.reshape(CHUNK // 8, 8, terms.shape[1]), axis=0)
            coef = jnp.where(codes > 0.5, sigmoid - jnp.where(matched, 1.0, 0.0), 0.0)
            coef = coef.astype(jnp.bfloat16)
            coef_ref[base + at : base + at + CHUNK] = coef
            sums_ref[at : at + CHUNK, :width] = jnp.dot(
                coef, group, preferred_element_type=jnp.float32
            )
    own_sums_ref[:, width:] = jnp.zeros((half, own_sums_ref.shape[1] - width), jnp.float32)
    loss_ref[...] = loss


def placed(value):
    return pltpu.with_memory_space_constraint(value, pltpu.VMEM)


def pair_terms(codes, parts, own_texts, other_texts):
    near, width = parts[0].shape
    half = own_texts.shape[0]
    images = SIDE * near
    return pl.pallas_call(
        pair_kernel,
        out_shape=(
            pltpu.VMEM((2 * half, images), jnp.bfloat16),
            pltpu.VMEM((half, width + SPARE), jnp.float32),
            pltpu.VMEM((half, width), jnp.float32),
            pltpu.VMEM((8, images), jnp.float32),
        ),
        in_specs=[VMEM] * (SIDE + 3),
        out_specs=(VMEM,) * 4,
        scratch_shapes=[pltpu.VMEM((images, width), jnp.bfloat16)],
        compiler_params=pltpu.CompilerParams(vmem_limit_bytes=20 * 2**20),
    )(*(placed(a) for a in (codes, *parts, own_texts, other_texts)))


def swapped(value):
    return lax.ppermute(value, "c", [(0, 1), (1, 0)])


def turned(value, axis, steps):
    return lax.ppermute(value, axis, [(k, (k + steps) % SIDE) for k in range(SIDE)])


def all_turned(block, axis):
    return [block] + [turned(block, axis, k) for k in range(1, SIDE)]


def turned_and_summed(parts, axis):
    sums = parts[0]
    got = [turned(parts[k].astype(jnp.float16), axis, -k) for k in range(1, SIDE)]
    for part in got:
        sums = sums + part.astype(jnp.float32)
    return sums


def over_image_group(total):
    axes = ("x", "za", "c")
    count = lax.axis_size(axes)
    sent = jnp.broadcast_to(total, (count, 8, 128))
    return jnp.sum(lax.all_to_all(sent, axes, 0, 0, tiled=True)[:, 0, 0])


def to_row(total, lanes, first):
    row = jnp.zeros(lanes.shape, jnp.float32)
    rest = total * (1.0 / TOP)
    for k in range(DIGITS):
        rest = rest * BASE
        digit = jnp.floor(rest)
        rest = rest - digit
        row = jnp.where(lanes == first + k, digit, row)
    return row


def from_row(row):
    worth = jnp.zeros(row.shape, jnp.float32)
    lanes = jnp.arange(row.shape[0], dtype=jnp.int32)
    for k in range(DIGITS):
        worth = jnp.where(lanes == k, TOP / BASE ** (k + 1), worth)
    return jnp.sum(row * worth)


def sent_and_summed(parts, axis):
    got = lax.all_to_all(parts, axis, 0, 0, tiled=True)
    return jnp.sum(got.astype(jnp.float32), axis=0)


def block_mask(tile_mask):
    x, zb, za, c, y = (lax.axis_index(n) for n in ("x", "zb", "za", "c", "y"))
    tiles = tile_mask.shape[0]

    def tile_of(xs, zbs, zas, cs, ys):
        return (((xs * 2 + zbs) * 4 + zas) * 2 + cs) * 2 + ys // 2

    k = jnp.arange(16, dtype=jnp.int32)
    image_tiles = tile_of((x - k // 4) % 4, zb, (za - k % 4) % 4, c, y)
    k = jnp.arange(32, dtype=jnp.int32)
    text_cores = jnp.where(k < 16, c, 1 - c)
    text_tiles = tile_of(x, k % 2, za, text_cores, (k // 4) % 4)
    every = jnp.arange(tiles, dtype=jnp.int32)
    left = (text_tiles[:, None] == every[None]).astype(jnp.float32)
    right = (image_tiles[:, None] == every[None]).astype(jnp.float32)
    chosen = lax.dot_general(right, tile_mask.astype(jnp.float32), (((1,), (0,)), ((), ())))
    return lax.dot_general(left, chosen, (((1,), (1,)), ((), ())))


def pair_codes(tile_mask, rows):
    own_text = lax.axis_index("y") * 4 + lax.axis_index(ZB)
    masked = block_mask(tile_mask)
    i = jnp.arange(16 * rows, dtype=jnp.int32)
    j = jnp.arange(32 * rows, dtype=jnp.int32)
    left = (j[:, None] // rows == jnp.arange(32)[None]).astype(jnp.float32)
    right = (jnp.arange(16)[:, None] == i[None] // rows).astype(jnp.float32)
    masked = jnp.dot(jnp.dot(left, masked), right)
    matched = i[None] == (j - own_text * rows)[:, None]
    matched = matched & (i < rows)[None]
    return jnp.where(matched, 2.0, jnp.where(masked < 0.5, 1.0, 0.0)).astype(jnp.bfloat16)


def back(values, inverse, grads):
    unit = values * inverse
    return inverse * (grads - unit * jnp.sum(unit * grads, axis=-1, keepdims=True))


def step(images, texts, tile_mask):
    rows, width = images.shape
    got = lax.all_to_all(normalized_slots(texts), ZB, 0, 0, tiled=True)
    images = images.astype(jnp.float32)
    texts = texts.astype(jnp.float32)
    image_inverse = inverse_norm(images)
    text_inverse = inverse_norm(texts)
    image_bf = (images * image_inverse).astype(jnp.bfloat16)
    near = all_turned(image_bf, "za")
    near = jnp.concatenate(near, axis=0)
    parts = all_turned(near, "x")
    sent = jnp.broadcast_to(got.reshape(1, SIDE * rows, width), (SIDE, SIDE * rows, width))
    own_texts = lax.all_to_all(sent, "y", 0, 0, tiled=True).reshape(16 * rows, width)
    other_texts = swapped(own_texts)
    codes = pair_codes(tile_mask, rows)

    coef, own_sums, other_sums, loss = pair_terms(codes, parts, own_texts, other_texts)
    other_sums = swapped(other_sums)
    loss = over_image_group(jnp.sum(loss))
    image_parts = lax.dot_general(
        coef[: 16 * rows], own_texts, (((0,), (0,)), ((), ())), preferred_element_type=jnp.float32
    ) + lax.dot_general(
        coef[16 * rows :], other_texts, (((0,), (0,)), ((), ())), preferred_element_type=jnp.float32
    )

    lanes = lax.broadcasted_iota(jnp.int32, (1, width + SPARE), 1)
    row = to_row(loss, lanes, width)
    text_parts = own_sums + jnp.pad(other_sums, ((0, 0), (0, SPARE)))
    text_parts = jnp.where(lanes >= width, row, text_parts).astype(jnp.float16)
    text_parts = sent_and_summed(text_parts.reshape(SIDE, SIDE * rows, -1), "y")
    image_parts = turned_and_summed(image_parts.reshape(SIDE, SIDE * rows, width), "x")
    text_parts = text_parts.astype(jnp.float16).reshape(SIDE, rows, -1)
    text_sums = sent_and_summed(text_parts, ZB)
    image_sums = turned_and_summed(image_parts.reshape(SIDE, rows, width), "za")
    loss = from_row(text_sums[0, width:])

    zero = tile_mask == 0
    size = tile_mask.shape[0]
    diagonal = jnp.eye(size, dtype=jnp.bool_)
    pairs = jnp.sum(jnp.where(zero, TILE * TILE, jnp.where(diagonal, TILE, 0)))
    return (
        back(images, image_inverse, TEMP * image_sums),
        back(texts, text_inverse, TEMP * text_sums[:, :width]),
        loss / pairs.astype(jnp.float32),
    )


def solution(mesh):
    finer = Mesh(mesh.devices.reshape(4, 2, 4, 2, 4, 2), ("y", "zh", "x", "zb", "za", "c"))
    placed = P(ROWS_AXES, None)
    return jax.shard_map(
        step,
        mesh=finer,
        in_specs=(placed, placed, P()),
        out_specs=(placed, placed, P()),
        check_vma=False,
    )
```

```python
import jax
import jax.numpy as jnp
from jax import lax
from jax.experimental import pallas as pl
from jax.experimental.pallas import tpu as pltpu
from jax.sharding import Mesh
from jax.sharding import PartitionSpec as P


TILE = 128
TEMP = 10.0
BIAS = -2.0
EPS = 1e-06
ROWS_AXES = ("x", "zb", "za", "c", "y", "zh")
ZB = ("zh", "zb")
IMAGE_GROUP = ("x", "za", "c")
SIDE = 4
DIGITS = 7
BASE = 512.0
TOP = 2.0**32
SPARE = 128
CHUNK = 256

VMEM = pl.BlockSpec(memory_space=pltpu.VMEM)


def inverse_norm(values):
    return lax.rsqrt(jnp.sum(values * values, axis=-1, keepdims=True) + EPS)


def slots_kernel(values_ref, slots_ref):
    values = values_ref[...].astype(jnp.float32)
    unit = (values * inverse_norm(values)).astype(jnp.bfloat16)
    for k in range(SIDE):
        slots_ref[k] = unit


def normalized_slots(values):
    return pl.pallas_call(
        slots_kernel,
        out_shape=pltpu.VMEM((SIDE, *values.shape), jnp.bfloat16),
        in_specs=[VMEM],
        out_specs=VMEM,
        compiler_params=pltpu.CompilerParams(vmem_limit_bytes=4 * 2**20),
    )(values)


def pair_kernel(own_text_ref, masked_ref, arrived_ref, *refs):
    del arrived_ref
    part_refs, (own_ref, other_ref) = refs[:SIDE], refs[SIDE : SIDE + 2]
    coef_ref, own_sums_ref, other_sums_ref, loss_ref, group_ref = refs[SIDE + 2 :]
    near = part_refs[0].shape[0]
    for k in range(SIDE):
        group_ref[k * near : (k + 1) * near] = part_refs[k][...]
    group = group_ref[...]
    images, _ = group.shape
    half = own_ref.shape[0]
    rows = 2 * half // masked_ref.shape[0]
    shape = (CHUNK, images)
    columns = lax.broadcasted_iota(jnp.int32, shape, 1)
    diagonal = columns - lax.broadcasted_iota(jnp.int32, shape, 0)
    loss = jnp.zeros((8, images), jnp.float32)
    for texts_ref, sums_ref, base in ((other_ref, other_sums_ref, half), (own_ref, own_sums_ref, 0)):
        for at in range(0, half, CHUNK):
            logits = TEMP * lax.dot_general(
                texts_ref[at : at + CHUNK],
                group,
                (((1,), (1,)), ((), ())),
                preferred_element_type=jnp.float32,
            )
            logits = logits + BIAS
            first = (base + at) // rows
            masked = masked_ref[first : first + CHUNK // rows]
            masked = jnp.broadcast_to(masked[:, None], (CHUNK // rows, rows, images)).reshape(shape)
            valid = masked < 0.5
            small = jnp.exp(-jnp.abs(logits))
            soft = jnp.maximum(logits, 0.0) + jnp.log1p(small)
            sigmoid = jnp.where(logits >= 0.0, 1.0, small) / (1.0 + small)
            if base == 0:
                matched = (diagonal == at - own_text_ref[0, 0] * rows) & (columns < rows)
                soft = soft - jnp.where(matched, logits, 0.0)
                sigmoid = sigmoid - jnp.where(matched, 1.0, 0.0)
                valid = valid | matched
            terms = jnp.where(valid, soft, 0.0)
            loss = loss + jnp.sum(terms.reshape(CHUNK // 8, 8, images), axis=0)
            coef = jnp.where(valid, sigmoid, 0.0).astype(jnp.bfloat16)
            coef_ref[base + at : base + at + CHUNK] = coef
            sums_ref[at : at + CHUNK] = jnp.dot(coef, group, preferred_element_type=jnp.float32)
    total = jnp.sum(jnp.sum(loss, axis=0, keepdims=True), axis=1, keepdims=True)
    loss_ref[...] = jnp.broadcast_to(total[None], loss_ref.shape)


def placed(value):
    return pltpu.with_memory_space_constraint(value, pltpu.VMEM)


def pair_terms(own_text, masked, arrived, parts, own_texts, other_texts, peers):
    near, width = parts[0].shape
    half = own_texts.shape[0]
    images = SIDE * near
    return pl.pallas_call(
        pair_kernel,
        out_shape=(
            jax.ShapeDtypeStruct((2 * half, images), jnp.bfloat16),
            jax.ShapeDtypeStruct((half, width), jnp.float32),
            pltpu.VMEM((half, width), jnp.float32),
            pltpu.VMEM((peers, 8, 128), jnp.float32),
        ),
        in_specs=[pl.BlockSpec(memory_space=pltpu.SMEM)] + [VMEM] * (SIDE + 4),
        out_specs=(VMEM,) * 4,
        scratch_shapes=[pltpu.VMEM((images, width), jnp.bfloat16)],
        compiler_params=pltpu.CompilerParams(vmem_limit_bytes=20 * 2**20),
    )(own_text, *(placed(a) for a in (masked, arrived, *parts, own_texts, other_texts)))


def swapped(value):
    return lax.ppermute(value, "c", [(0, 1), (1, 0)])


def turned(value, axis, steps):
    return lax.ppermute(value, axis, [(k, (k + steps) % SIDE) for k in range(SIDE)])


def all_turned(block, axis):
    return [block] + [turned(block, axis, k) for k in range(1, SIDE)]


def turned_and_summed(parts, axis):
    sums = parts[0]
    got = [turned(parts[k].astype(jnp.float16), axis, -k) for k in range(1, SIDE)]
    for part in got:
        sums = sums + part.astype(jnp.float32)
    return lax.optimization_barrier(sums)


def to_row(total, lanes, first):
    row = jnp.zeros(lanes.shape, jnp.float32)
    rest = total * (1.0 / TOP)
    for k in range(DIGITS):
        rest = rest * BASE
        digit = jnp.floor(rest)
        rest = rest - digit
        row = jnp.where(lanes == first + k, digit, row)
    return row


def from_row(row):
    worth = jnp.zeros(row.shape, jnp.float32)
    lanes = jnp.arange(row.shape[0], dtype=jnp.int32)
    for k in range(DIGITS):
        worth = jnp.where(lanes == k, TOP / BASE ** (k + 1), worth)
    return jnp.sum(row * worth)


def sent_and_summed(parts, axis):
    got = lax.all_to_all(parts, axis, 0, 0, tiled=True)
    return jnp.sum(got.astype(jnp.float32), axis=0)


def block_mask(tile_mask):
    x, zb, za, c, y = (lax.axis_index(n) for n in ("x", "zb", "za", "c", "y"))
    tiles = tile_mask.shape[0]

    def tile_of(xs, zbs, zas, cs, ys):
        return (((xs * 2 + zbs) * 4 + zas) * 2 + cs) * 2 + ys // 2

    k = jnp.arange(16, dtype=jnp.int32)
    image_tiles = tile_of((x - k // 4) % 4, zb, (za - k % 4) % 4, c, y)
    k = jnp.arange(32, dtype=jnp.int32)
    text_cores = jnp.where(k < 16, c, 1 - c)
    text_tiles = tile_of(x, k % 2, za, text_cores, (k // 4) % 4)
    every = jnp.arange(tiles, dtype=jnp.int32)
    left = (text_tiles[:, None] == every[None]).astype(jnp.float32)
    right = (image_tiles[:, None] == every[None]).astype(jnp.float32)
    chosen = lax.dot_general(right, tile_mask.astype(jnp.float32), (((1,), (0,)), ((), ())))
    return lax.dot_general(left, chosen, (((1,), (1,)), ((), ())))


def mask_rows(tile_mask, rows):
    i = jnp.arange(16 * rows, dtype=jnp.int32)
    right = (jnp.arange(16)[:, None] == i[None] // rows).astype(jnp.float32)
    return jnp.dot(block_mask(tile_mask), right)


def back(values, inverse, grads):
    unit = values * inverse
    return inverse * (grads - unit * jnp.sum(unit * grads, axis=-1, keepdims=True))


def step(images, texts, tile_mask):
    rows, width = images.shape
    got = lax.all_to_all(normalized_slots(texts), ZB, 0, 0, tiled=True)
    images = images.astype(jnp.float32)
    texts = texts.astype(jnp.float32)
    image_inverse = inverse_norm(images)
    text_inverse = inverse_norm(texts)
    image_bf = (images * image_inverse).astype(jnp.bfloat16)
    near = all_turned(image_bf, "za")
    near = jnp.concatenate(near, axis=0)
    parts = all_turned(near, "x")
    sent = jnp.broadcast_to(got.reshape(1, SIDE * rows, width), (SIDE, SIDE * rows, width))
    own_texts = lax.all_to_all(sent, "y", 0, 0, tiled=True).reshape(16 * rows, width)
    other_texts = swapped(own_texts)
    arrived = parts[1][:16, :128] + parts[2][:16, :128] + parts[3][:16, :128]
    masked = mask_rows(tile_mask, rows)
    own_text = (lax.axis_index("y") * SIDE + lax.axis_index(ZB)).reshape(1, 1)
    peers = lax.axis_size(IMAGE_GROUP)
    coef, own_sums, other_sums, loss = pair_terms(
        own_text, masked, arrived, parts, own_texts, other_texts, peers
    )
    other_sums = swapped(other_sums)
    loss = lax.all_to_all(loss, IMAGE_GROUP, 0, 0, tiled=True)
    loss = jnp.sum(loss[:, 0, 0])
    image_parts = lax.dot_general(
        coef[: 16 * rows], own_texts, (((0,), (0,)), ((), ())), preferred_element_type=jnp.float32
    ) + lax.dot_general(
        coef[16 * rows :], other_texts, (((0,), (0,)), ((), ())), preferred_element_type=jnp.float32
    )
    payload = jnp.pad((own_sums + other_sums).astype(jnp.float16), ((0, 0), (0, SPARE)))
    payload = lax.optimization_barrier(payload)
    lanes = lax.broadcasted_iota(jnp.int32, (1, SPARE), 1)
    row = to_row(loss, lanes, 0).astype(jnp.float16)
    payload = lax.dynamic_update_slice(
        payload, jnp.broadcast_to(row, (payload.shape[0], SPARE)), (0, width)
    )
    text_parts = sent_and_summed(payload.reshape(SIDE, SIDE * rows, -1), "y")
    image_parts = turned_and_summed(image_parts.reshape(SIDE, SIDE * rows, width), "x")
    text_parts = text_parts.astype(jnp.float16).reshape(SIDE, rows, -1)
    text_sums = sent_and_summed(text_parts, ZB)
    image_sums = turned_and_summed(image_parts.reshape(SIDE, rows, width), "za")
    loss = from_row(text_sums[0, width:])

    zero = tile_mask == 0
    size = tile_mask.shape[0]
    diagonal = jnp.eye(size, dtype=jnp.bool_)
    pairs = jnp.sum(jnp.where(zero, TILE * TILE, jnp.where(diagonal, TILE, 0)))
    return (
        back(images, image_inverse, TEMP * image_sums),
        back(texts, text_inverse, TEMP * text_sums[:, :width]),
        loss / pairs.astype(jnp.float32),
    )


def solution(mesh):
    finer = Mesh(mesh.devices.reshape(4, 2, 4, 2, 4, 2), ("y", "zh", "x", "zb", "za", "c"))
    placed = P(ROWS_AXES, None)
    return jax.shard_map(
        step,
        mesh=finer,
        in_specs=(placed, placed, P()),
        out_specs=(placed, placed, P()),
        check_vma=False,
    )
```

```python
import jax
import jax.numpy as jnp
from jax import lax
from jax.experimental import pallas as pl
from jax.experimental.pallas import tpu as pltpu
from jax.sharding import Mesh
from jax.sharding import PartitionSpec as P


TILE = 128
TEMP = 10.0
BIAS = -2.0
EPS = 1e-06
ROWS_AXES = ("x", "zb", "za", "c", "y", "zh")
ZB = ("zh", "zb")
IMAGE_GROUP = ("x", "za", "c")
SIDE = 4
DIGITS = 7
BASE = 512.0
TOP = 2.0**32
SPARE = 128
CHUNK = 256

VMEM = pl.BlockSpec(memory_space=pltpu.VMEM)


def inverse_norm(values):
    return lax.rsqrt(jnp.sum(values * values, axis=-1, keepdims=True) + EPS)


def slots_kernel(values_ref, slots_ref):
    values = values_ref[...].astype(jnp.float32)
    unit = (values * inverse_norm(values)).astype(jnp.bfloat16)
    for k in range(SIDE):
        slots_ref[k] = unit


def normalized_slots(values):
    return pl.pallas_call(
        slots_kernel,
        out_shape=pltpu.VMEM((SIDE, *values.shape), jnp.bfloat16),
        in_specs=[VMEM],
        out_specs=VMEM,
        compiler_params=pltpu.CompilerParams(vmem_limit_bytes=4 * 2**20),
    )(values)


def pair_kernel(own_text_ref, masked_ref, arrived_ref, *refs):
    del arrived_ref
    part_refs, (own_ref, other_ref) = refs[:SIDE], refs[SIDE : SIDE + 2]
    coef_ref, loss_ref, group_ref = refs[SIDE + 2 :]
    near = part_refs[0].shape[0]
    for k in range(SIDE):
        group_ref[k * near : (k + 1) * near] = part_refs[k][...]
    group = group_ref[...]
    images, _ = group.shape
    half = own_ref.shape[0]
    rows = 2 * half // masked_ref.shape[0]
    shape = (CHUNK, images)
    columns = lax.broadcasted_iota(jnp.int32, shape, 1)
    diagonal = columns - lax.broadcasted_iota(jnp.int32, shape, 0)
    loss = jnp.zeros((8, images), jnp.float32)
    for texts_ref, base in ((other_ref, half), (own_ref, 0)):
        for at in range(0, half, CHUNK):
            logits = TEMP * lax.dot_general(
                texts_ref[at : at + CHUNK],
                group,
                (((1,), (1,)), ((), ())),
                preferred_element_type=jnp.float32,
            )
            logits = logits + BIAS
            first = (base + at) // rows
            masked = masked_ref[first : first + CHUNK // rows]
            masked = jnp.broadcast_to(masked[:, None], (CHUNK // rows, rows, images)).reshape(shape)
            valid = masked < 0.5
            small = jnp.exp(-jnp.abs(logits))
            soft = jnp.maximum(logits, 0.0) + jnp.log1p(small)
            sigmoid = jnp.where(logits >= 0.0, 1.0, small) / (1.0 + small)
            if base == 0:
                matched = (diagonal == at - own_text_ref[0, 0] * rows) & (columns < rows)
                soft = soft - jnp.where(matched, logits, 0.0)
                sigmoid = sigmoid - jnp.where(matched, 1.0, 0.0)
                valid = valid | matched
            terms = jnp.where(valid, soft, 0.0)
            loss = loss + jnp.sum(terms.reshape(CHUNK // 8, 8, images), axis=0)
            coef = jnp.where(valid, sigmoid, 0.0).astype(jnp.bfloat16)
            coef_ref[base + at : base + at + CHUNK] = coef
    total = jnp.sum(jnp.sum(loss, axis=0, keepdims=True), axis=1, keepdims=True)
    loss_ref[...] = jnp.broadcast_to(total[None], loss_ref.shape)


def pair_terms(own_text, masked, arrived, parts, own_texts, other_texts, peers):
    near, width = parts[0].shape
    half = own_texts.shape[0]
    images = SIDE * near
    return pl.pallas_call(
        pair_kernel,
        out_shape=(
            pltpu.HBM((2 * half, images), jnp.bfloat16),
            pltpu.HBM((peers, 8, 128), jnp.float32),
            jax.ShapeDtypeStruct((images, width), jnp.bfloat16),
        ),
        in_specs=[pl.BlockSpec(memory_space=pltpu.SMEM)] + [VMEM] * (SIDE + 4),
        out_specs=(VMEM,) * 3,
        compiler_params=pltpu.CompilerParams(vmem_limit_bytes=20 * 2**20),
    )(own_text, masked, arrived, *parts, own_texts, other_texts)


def swapped(value):
    return lax.ppermute(value, "c", [(0, 1), (1, 0)])


def turned(value, axis, steps):
    return lax.ppermute(value, axis, [(k, (k + steps) % SIDE) for k in range(SIDE)])


def all_turned(block, axis):
    return [block] + [turned(block, axis, k) for k in range(1, SIDE)]


def turned_and_summed(parts, axis):
    sums = parts[0]
    got = [turned(parts[k].astype(jnp.float16), axis, -k) for k in range(1, SIDE)]
    for part in got:
        sums = sums + part.astype(jnp.float32)
    return lax.optimization_barrier(sums)


def digits_kernel(got_ref, row_ref):
    rest = jnp.sum(got_ref[...], axis=0) * (1.0 / TOP)
    lanes = lax.broadcasted_iota(jnp.int32, rest.shape, 1)
    row = jnp.zeros(rest.shape, jnp.float32)
    for k in range(DIGITS):
        rest = rest * BASE
        digit = jnp.floor(rest)
        rest = rest - digit
        row = jnp.where(lanes == k, digit, row)
    row_ref[...] = row


def digit_row(got):
    return pl.pallas_call(
        digits_kernel,
        out_shape=jax.ShapeDtypeStruct(got.shape[1:], jnp.float32),
        in_specs=[VMEM],
        out_specs=VMEM,
        compiler_params=pltpu.CompilerParams(vmem_limit_bytes=4 * 2**20),
    )(got)[:1]


def from_row(row):
    worth = jnp.zeros(row.shape, jnp.float32)
    lanes = jnp.arange(row.shape[0], dtype=jnp.int32)
    for k in range(DIGITS):
        worth = jnp.where(lanes == k, TOP / BASE ** (k + 1), worth)
    return jnp.sum(row * worth)


def sent_and_summed(parts, axis):
    got = lax.all_to_all(parts, axis, 0, 0, tiled=True)
    sums = got[0].astype(jnp.float32)
    for k in range(1, SIDE):
        sums = sums + got[k].astype(jnp.float32)
    return sums


def block_mask(tile_mask):
    x, zb, za, c, y = (lax.axis_index(n) for n in ("x", "zb", "za", "c", "y"))
    tiles = tile_mask.shape[0]

    def tile_of(xs, zbs, zas, cs, ys):
        return (((xs * 2 + zbs) * 4 + zas) * 2 + cs) * 2 + ys // 2

    k = jnp.arange(16, dtype=jnp.int32)
    image_tiles = tile_of((x - k // 4) % 4, zb, (za - k % 4) % 4, c, y)
    k = jnp.arange(32, dtype=jnp.int32)
    text_cores = jnp.where(k < 16, c, 1 - c)
    text_tiles = tile_of(x, k % 2, za, text_cores, (k // 4) % 4)
    every = jnp.arange(tiles, dtype=jnp.int32)
    left = (text_tiles[:, None] == every[None]).astype(jnp.float32)
    right = (image_tiles[:, None] == every[None]).astype(jnp.float32)
    chosen = lax.dot_general(right, tile_mask.astype(jnp.float32), (((1,), (0,)), ((), ())))
    return lax.dot_general(left, chosen, (((1,), (1,)), ((), ())))


def mask_rows(tile_mask, rows):
    i = jnp.arange(16 * rows, dtype=jnp.int32)
    right = (jnp.arange(16)[:, None] == i[None] // rows).astype(jnp.float32)
    return jnp.dot(block_mask(tile_mask), right)


def back(values, inverse, grads):
    unit = values * inverse
    return inverse * (grads - unit * jnp.sum(unit * grads, axis=-1, keepdims=True))


def step(images, texts, tile_mask):
    rows, width = images.shape
    got = lax.all_to_all(normalized_slots(texts), ZB, 0, 0, tiled=True)
    images = images.astype(jnp.float32)
    texts = texts.astype(jnp.float32)
    image_inverse = inverse_norm(images)
    text_inverse = inverse_norm(texts)
    image_bf = (images * image_inverse).astype(jnp.bfloat16)
    near = all_turned(image_bf, "za")
    near = jnp.concatenate(near, axis=0)
    parts = all_turned(near, "x")
    sent = jnp.broadcast_to(got.reshape(1, SIDE * rows, width), (SIDE, SIDE * rows, width))
    own_texts = lax.all_to_all(sent, "y", 0, 0, tiled=True).reshape(16 * rows, width)
    other_texts = swapped(own_texts)
    arrived = parts[1][:16, :128] + parts[2][:16, :128] + parts[3][:16, :128]
    masked = mask_rows(tile_mask, rows)
    own_text = (lax.axis_index("y") * SIDE + lax.axis_index(ZB)).reshape(1, 1)
    peers = lax.axis_size(IMAGE_GROUP)
    coef, loss, group = pair_terms(
        own_text, masked, arrived, parts, own_texts, other_texts, peers
    )
    loss = lax.all_to_all(loss, IMAGE_GROUP, 0, 0, tiled=True)
    other_sums = jnp.dot(coef[16 * rows :], group, preferred_element_type=jnp.float32)
    other_sums = swapped(other_sums)
    image_parts = lax.dot_general(
        coef[: 16 * rows], own_texts, (((0,), (0,)), ((), ())), preferred_element_type=jnp.float32
    ) + lax.dot_general(
        coef[16 * rows :], other_texts, (((0,), (0,)), ((), ())), preferred_element_type=jnp.float32
    )
    own_sums = jnp.dot(coef[: 16 * rows], group, preferred_element_type=jnp.float32)
    payload = lax.optimization_barrier((own_sums + other_sums).astype(jnp.float16))
    row = digit_row(loss)
    lanes = lax.broadcasted_iota(jnp.int32, (1, width + SPARE), 1)
    row = jnp.pad(row, ((0, 0), (width, 0))).astype(jnp.float16)
    payload = jnp.where(lanes >= width, row, jnp.pad(payload, ((0, 0), (0, SPARE))))
    text_parts = sent_and_summed(payload.reshape(SIDE, SIDE * rows, -1), "y")
    image_parts = turned_and_summed(image_parts.reshape(SIDE, SIDE * rows, width), "x")
    text_parts = text_parts.astype(jnp.float16).reshape(SIDE, rows, -1)
    text_sums = sent_and_summed(text_parts, ZB)
    image_sums = turned_and_summed(image_parts.reshape(SIDE, rows, width), "za")
    loss = from_row(text_sums[0, width:])

    zero = tile_mask == 0
    size = tile_mask.shape[0]
    diagonal = jnp.eye(size, dtype=jnp.bool_)
    pairs = jnp.sum(jnp.where(zero, TILE * TILE, jnp.where(diagonal, TILE, 0)))
    return (
        back(images, image_inverse, TEMP * image_sums),
        back(texts, text_inverse, TEMP * text_sums[:, :width]),
        loss / pairs.astype(jnp.float32),
    )


def solution(mesh):
    finer = Mesh(mesh.devices.reshape(4, 2, 4, 2, 4, 2), ("y", "zh", "x", "zb", "za", "c"))
    placed = P(ROWS_AXES, None)
    return jax.shard_map(
        step,
        mesh=finer,
        in_specs=(placed, placed, P()),
        out_specs=(placed, placed, P()),
        check_vma=False,
    )
```

```python
import jax
import jax.numpy as jnp
from jax import lax
from jax.experimental import pallas as pl
from jax.experimental.pallas import tpu as pltpu
from jax.sharding import Mesh
from jax.sharding import PartitionSpec as P


TILE = 128
TEMP = 10.0
BIAS = -2.0
EPS = 1e-06
ROWS_AXES = ("x", "zb", "za", "c", "y", "zh")
ZB = ("zh", "zb")
IMAGE_GROUP = ("x", "za", "c")
SIDE = 4
DIGITS = 7
BASE = 512.0
TOP = 2.0**32
SPARE = 128
CHUNK = 256

VMEM = pl.BlockSpec(memory_space=pltpu.VMEM)
HBM = pl.BlockSpec(memory_space=pltpu.HBM)


def inverse_norm(values):
    return lax.rsqrt(jnp.sum(values * values, axis=-1, keepdims=True) + EPS)


def slots_kernel(values_ref, slots_ref):
    values = values_ref[...].astype(jnp.float32)
    unit = (values * inverse_norm(values)).astype(jnp.bfloat16)
    for k in range(SIDE):
        slots_ref[k] = unit


def normalized_slots(values):
    return pl.pallas_call(
        slots_kernel,
        out_shape=pltpu.VMEM((SIDE, *values.shape), jnp.bfloat16),
        in_specs=[VMEM],
        out_specs=VMEM,
        compiler_params=pltpu.CompilerParams(vmem_limit_bytes=4 * 2**20),
    )(values)


def pair_kernel(own_text_ref, masked_hbm_ref, *refs):
    part_refs, (own_ref, other_ref) = refs[:SIDE], refs[SIDE : SIDE + 2]
    coef_ref, loss_ref, group_ref, masked_ref, arrived = refs[SIDE + 2 :]
    near = part_refs[0].shape[0]
    copies = [
        pltpu.make_async_copy(part_refs[k], group_ref.at[pl.ds(k * near, near)], arrived.at[k])
        for k in range(SIDE)
    ]
    copies.append(pltpu.make_async_copy(masked_hbm_ref, masked_ref, arrived.at[SIDE]))
    for copy in copies:
        copy.start()
    for copy in copies:
        copy.wait()
    group = group_ref[...]
    images, _ = group.shape
    half = own_ref.shape[0]
    rows = 2 * half // masked_ref.shape[0]
    shape = (CHUNK, images)
    columns = lax.broadcasted_iota(jnp.int32, shape, 1)
    diagonal = columns - lax.broadcasted_iota(jnp.int32, shape, 0)
    loss = jnp.zeros((8, images), jnp.float32)
    for texts_ref, base in ((other_ref, half), (own_ref, 0)):
        for at in range(0, half, CHUNK):
            logits = TEMP * lax.dot_general(
                texts_ref[at : at + CHUNK],
                group,
                (((1,), (1,)), ((), ())),
                preferred_element_type=jnp.float32,
            )
            logits = logits + BIAS
            first = (base + at) // rows
            masked = masked_ref[first : first + CHUNK // rows]
            masked = jnp.broadcast_to(masked[:, None], (CHUNK // rows, rows, images)).reshape(shape)
            valid = masked < 0.5
            small = jnp.exp(-jnp.abs(logits))
            soft = jnp.maximum(logits, 0.0) + jnp.log1p(small)
            sigmoid = jnp.where(logits >= 0.0, 1.0, small) / (1.0 + small)
            if base == 0:
                matched = (diagonal == at - own_text_ref[0, 0] * rows) & (columns < rows)
                soft = soft - jnp.where(matched, logits, 0.0)
                sigmoid = sigmoid - jnp.where(matched, 1.0, 0.0)
                valid = valid | matched
            terms = jnp.where(valid, soft, 0.0)
            loss = loss + jnp.sum(terms.reshape(CHUNK // 8, 8, images), axis=0)
            coef = jnp.where(valid, sigmoid, 0.0).astype(jnp.bfloat16)
            coef_ref[base + at : base + at + CHUNK] = coef
    total = jnp.sum(jnp.sum(loss, axis=0, keepdims=True), axis=1, keepdims=True)
    loss_ref[...] = jnp.broadcast_to(total[None], loss_ref.shape)


def held(value):
    return pltpu.with_memory_space_constraint(value, pltpu.HBM)


def pair_terms(own_text, masked, parts, own_texts, other_texts, peers):
    near, width = parts[0].shape
    half = own_texts.shape[0]
    images = SIDE * near
    return pl.pallas_call(
        pair_kernel,
        out_shape=(
            pltpu.HBM((2 * half, images), jnp.bfloat16),
            pltpu.HBM((peers, 8, 128), jnp.float32),
            jax.ShapeDtypeStruct((images, width), jnp.bfloat16),
        ),
        in_specs=[pl.BlockSpec(memory_space=pltpu.SMEM)] + [HBM] * (SIDE + 1) + [VMEM] * 2,
        out_specs=(VMEM,) * 3,
        scratch_shapes=[
            pltpu.VMEM(masked.shape, jnp.float32),
            pltpu.SemaphoreType.DMA((SIDE + 1,)),
        ],
        compiler_params=pltpu.CompilerParams(vmem_limit_bytes=20 * 2**20),
    )(own_text, *(held(a) for a in (masked, *parts)), own_texts, other_texts)


def swapped(value):
    return lax.ppermute(value, "c", [(0, 1), (1, 0)])


def turned(value, axis, steps):
    return lax.ppermute(value, axis, [(k, (k + steps) % SIDE) for k in range(SIDE)])


def all_turned(block, axis):
    return [block] + [turned(block, axis, k) for k in range(1, SIDE)]


def turned_and_summed(parts, axis):
    sums = parts[0]
    got = [turned(parts[k].astype(jnp.float16), axis, -k) for k in range(1, SIDE)]
    for part in got:
        sums = sums + part.astype(jnp.float32)
    return lax.optimization_barrier(sums)


def digits_kernel(got_ref, row_ref):
    rest = jnp.sum(got_ref[...], axis=0) * (1.0 / TOP)
    lanes = lax.broadcasted_iota(jnp.int32, rest.shape, 1)
    row = jnp.zeros(rest.shape, jnp.float32)
    for k in range(DIGITS):
        rest = rest * BASE
        digit = jnp.floor(rest)
        rest = rest - digit
        row = jnp.where(lanes == k, digit, row)
    row_ref[...] = row


def digit_row(got):
    return pl.pallas_call(
        digits_kernel,
        out_shape=jax.ShapeDtypeStruct(got.shape[1:], jnp.float32),
        in_specs=[VMEM],
        out_specs=VMEM,
        compiler_params=pltpu.CompilerParams(vmem_limit_bytes=4 * 2**20),
    )(got)[:1]


def from_row(row):
    worth = jnp.zeros(row.shape, jnp.float32)
    lanes = jnp.arange(row.shape[0], dtype=jnp.int32)
    for k in range(DIGITS):
        worth = jnp.where(lanes == k, TOP / BASE ** (k + 1), worth)
    return jnp.sum(row * worth)


def sent_and_summed(parts, axis):
    got = lax.all_to_all(parts, axis, 0, 0, tiled=True)
    sums = got[0].astype(jnp.float32)
    for k in range(1, SIDE):
        sums = sums + got[k].astype(jnp.float32)
    return sums


def block_mask(tile_mask):
    x, zb, za, c, y = (lax.axis_index(n) for n in ("x", "zb", "za", "c", "y"))
    tiles = tile_mask.shape[0]

    def tile_of(xs, zbs, zas, cs, ys):
        return (((xs * 2 + zbs) * 4 + zas) * 2 + cs) * 2 + ys // 2

    k = jnp.arange(16, dtype=jnp.int32)
    image_tiles = tile_of((x - k // 4) % 4, zb, (za - k % 4) % 4, c, y)
    k = jnp.arange(32, dtype=jnp.int32)
    text_cores = jnp.where(k < 16, c, 1 - c)
    text_tiles = tile_of(x, k % 2, za, text_cores, (k // 4) % 4)
    every = jnp.arange(tiles, dtype=jnp.int32)
    left = (text_tiles[:, None] == every[None]).astype(jnp.float32)
    right = (image_tiles[:, None] == every[None]).astype(jnp.float32)
    chosen = lax.dot_general(right, tile_mask.astype(jnp.float32), (((1,), (0,)), ((), ())))
    return lax.dot_general(left, chosen, (((1,), (1,)), ((), ())))


def mask_rows(tile_mask, rows):
    i = jnp.arange(16 * rows, dtype=jnp.int32)
    right = (jnp.arange(16)[:, None] == i[None] // rows).astype(jnp.float32)
    return jnp.dot(block_mask(tile_mask), right)


def back(values, inverse, grads):
    unit = values * inverse
    return inverse * (grads - unit * jnp.sum(unit * grads, axis=-1, keepdims=True))


def step(images, texts, tile_mask):
    rows, width = images.shape
    got = lax.all_to_all(normalized_slots(texts), ZB, 0, 0, tiled=True)
    images = images.astype(jnp.float32)
    texts = texts.astype(jnp.float32)
    image_inverse = inverse_norm(images)
    text_inverse = inverse_norm(texts)
    image_bf = (images * image_inverse).astype(jnp.bfloat16)
    near = all_turned(image_bf, "za")
    near = jnp.concatenate(near, axis=0)
    parts = all_turned(near, "x")
    sent = jnp.broadcast_to(got.reshape(1, SIDE * rows, width), (SIDE, SIDE * rows, width))
    own_texts = lax.all_to_all(sent, "y", 0, 0, tiled=True).reshape(16 * rows, width)
    other_texts = swapped(own_texts)
    masked = mask_rows(tile_mask, rows)
    own_text = (lax.axis_index("y") * SIDE + lax.axis_index(ZB)).reshape(1, 1)
    peers = lax.axis_size(IMAGE_GROUP)
    coef, loss, group = pair_terms(
        own_text, masked, parts, own_texts, other_texts, peers
    )
    loss = lax.all_to_all(loss, IMAGE_GROUP, 0, 0, tiled=True)
    other_sums = jnp.dot(coef[16 * rows :], group, preferred_element_type=jnp.float32)
    other_sums = swapped(other_sums)
    image_parts = lax.dot_general(
        coef[: 16 * rows], own_texts, (((0,), (0,)), ((), ())), preferred_element_type=jnp.float32
    ) + lax.dot_general(
        coef[16 * rows :], other_texts, (((0,), (0,)), ((), ())), preferred_element_type=jnp.float32
    )
    own_sums = jnp.dot(coef[: 16 * rows], group, preferred_element_type=jnp.float32)
    payload = lax.optimization_barrier((own_sums + other_sums).astype(jnp.float16))
    row = digit_row(loss)
    lanes = lax.broadcasted_iota(jnp.int32, (1, width + SPARE), 1)
    row = jnp.pad(row, ((0, 0), (width, 0))).astype(jnp.float16)
    payload = jnp.where(lanes >= width, row, jnp.pad(payload, ((0, 0), (0, SPARE))))
    text_parts = sent_and_summed(payload.reshape(SIDE, SIDE * rows, -1), "y")
    image_parts = turned_and_summed(image_parts.reshape(SIDE, SIDE * rows, width), "x")
    text_parts = text_parts.astype(jnp.float16).reshape(SIDE, rows, -1)
    text_sums = sent_and_summed(text_parts, ZB)
    image_sums = turned_and_summed(image_parts.reshape(SIDE, rows, width), "za")
    loss = from_row(text_sums[0, width:])

    zero = tile_mask == 0
    size = tile_mask.shape[0]
    diagonal = jnp.eye(size, dtype=jnp.bool_)
    pairs = jnp.sum(jnp.where(zero, TILE * TILE, jnp.where(diagonal, TILE, 0)))
    return (
        back(images, image_inverse, TEMP * image_sums),
        back(texts, text_inverse, TEMP * text_sums[:, :width]),
        loss / pairs.astype(jnp.float32),
    )


def solution(mesh):
    finer = Mesh(mesh.devices.reshape(4, 2, 4, 2, 4, 2), ("y", "zh", "x", "zb", "za", "c"))
    placed = P(ROWS_AXES, None)
    return jax.shard_map(
        step,
        mesh=finer,
        in_specs=(placed, placed, P()),
        out_specs=(placed, placed, P()),
        check_vma=False,
    )
```

```python
import jax
import jax.numpy as jnp
from jax import lax
from jax.experimental import pallas as pl
from jax.experimental.pallas import tpu as pltpu
from jax.sharding import Mesh
from jax.sharding import PartitionSpec as P


TILE = 128
TEMP = 10.0
BIAS = -2.0
EPS = 1e-06
ROWS_AXES = ("x", "zb", "za", "c", "y", "zh")
ZB = ("zh", "zb")
IMAGE_GROUP = ("x", "za", "c")
SIDE = 4
DIGITS = 7
BASE = 512.0
TOP = 2.0**32
SPARE = 128
CHUNK = 256

VMEM = pl.BlockSpec(memory_space=pltpu.VMEM)
HBM = pl.BlockSpec(memory_space=pltpu.HBM)


def inverse_norm(values):
    return lax.rsqrt(jnp.sum(values * values, axis=-1, keepdims=True) + EPS)


def held(value):
    return pltpu.with_memory_space_constraint(value, pltpu.HBM)


def slots_kernel(texts_hbm_ref, images_hbm_ref, slots_ref, images_ref, fetched_ref, arrived):
    copies = [
        pltpu.make_async_copy(source, fetched_ref.at[k], arrived.at[k])
        for k, source in enumerate((texts_hbm_ref, images_hbm_ref))
    ]
    for copy in copies:
        copy.start()
    units = []
    for k, copy in enumerate(copies):
        copy.wait()
        values = fetched_ref[k].astype(jnp.float32)
        units.append((values * inverse_norm(values)).astype(jnp.bfloat16))
    for k in range(SIDE):
        slots_ref[k] = units[0]
    images_ref[...] = units[1]


def normalized(texts, images):
    return pl.pallas_call(
        slots_kernel,
        out_shape=(
            jax.ShapeDtypeStruct((SIDE, *texts.shape), jnp.bfloat16),
            jax.ShapeDtypeStruct(images.shape, jnp.bfloat16),
        ),
        in_specs=[HBM] * 2,
        out_specs=(VMEM,) * 2,
        scratch_shapes=[
            pltpu.VMEM((2, *texts.shape), jnp.bfloat16),
            pltpu.SemaphoreType.DMA((2,)),
        ],
        compiler_params=pltpu.CompilerParams(vmem_limit_bytes=4 * 2**20),
    )(held(texts), held(images))


def pair_kernel(own_text_ref, masked_hbm_ref, *refs):
    part_refs, (own_ref, other_ref) = refs[:SIDE], refs[SIDE : SIDE + 2]
    coef_ref, loss_ref, group_ref, masked_ref, arrived = refs[SIDE + 2 :]
    near = part_refs[0].shape[0]
    copies = [
        pltpu.make_async_copy(part_refs[k], group_ref.at[pl.ds(k * near, near)], arrived.at[k])
        for k in range(SIDE)
    ]
    copies.append(pltpu.make_async_copy(masked_hbm_ref, masked_ref, arrived.at[SIDE]))
    for copy in copies:
        copy.start()
    for copy in copies:
        copy.wait()
    group = group_ref[...]
    images, _ = group.shape
    half = own_ref.shape[0]
    rows = 2 * half // masked_ref.shape[0]
    shape = (CHUNK, images)
    columns = lax.broadcasted_iota(jnp.int32, shape, 1)
    diagonal = columns - lax.broadcasted_iota(jnp.int32, shape, 0)
    loss = jnp.zeros((8, images), jnp.float32)
    for texts_ref, base in ((other_ref, half), (own_ref, 0)):
        for at in range(0, half, CHUNK):
            logits = TEMP * lax.dot_general(
                texts_ref[at : at + CHUNK],
                group,
                (((1,), (1,)), ((), ())),
                preferred_element_type=jnp.float32,
            )
            logits = logits + BIAS
            first = (base + at) // rows
            masked = masked_ref[first : first + CHUNK // rows]
            masked = jnp.broadcast_to(masked[:, None], (CHUNK // rows, rows, images)).reshape(shape)
            valid = masked < 0.5
            small = jnp.exp(-jnp.abs(logits))
            soft = jnp.maximum(logits, 0.0) + jnp.log1p(small)
            sigmoid = jnp.where(logits >= 0.0, 1.0, small) / (1.0 + small)
            if base == 0:
                matched = (diagonal == at - own_text_ref[0, 0] * rows) & (columns < rows)
                soft = soft - jnp.where(matched, logits, 0.0)
                sigmoid = sigmoid - jnp.where(matched, 1.0, 0.0)
                valid = valid | matched
            terms = jnp.where(valid, soft, 0.0)
            loss = loss + jnp.sum(terms.reshape(CHUNK // 8, 8, images), axis=0)
            coef = jnp.where(valid, sigmoid, 0.0).astype(jnp.bfloat16)
            coef_ref[base + at : base + at + CHUNK] = coef
    total = jnp.sum(jnp.sum(loss, axis=0, keepdims=True), axis=1, keepdims=True)
    loss_ref[...] = jnp.broadcast_to(total[None], loss_ref.shape)


def pair_terms(own_text, masked, parts, own_texts, other_texts, peers):
    near, width = parts[0].shape
    half = own_texts.shape[0]
    images = SIDE * near
    return pl.pallas_call(
        pair_kernel,
        out_shape=(
            pltpu.HBM((2 * half, images), jnp.bfloat16),
            pltpu.HBM((peers, 8, 128), jnp.float32),
            jax.ShapeDtypeStruct((images, width), jnp.bfloat16),
        ),
        in_specs=[pl.BlockSpec(memory_space=pltpu.SMEM)] + [HBM] * (SIDE + 1) + [VMEM] * 2,
        out_specs=(VMEM,) * 3,
        scratch_shapes=[
            pltpu.VMEM(masked.shape, jnp.float32),
            pltpu.SemaphoreType.DMA((SIDE + 1,)),
        ],
        compiler_params=pltpu.CompilerParams(vmem_limit_bytes=20 * 2**20),
    )(own_text, *(held(a) for a in (masked, *parts)), own_texts, other_texts)


def swapped(value):
    return lax.ppermute(value, "c", [(0, 1), (1, 0)])


def turned(value, axis, steps):
    return lax.ppermute(value, axis, [(k, (k + steps) % SIDE) for k in range(SIDE)])


def all_turned(block, axis):
    return [block] + [turned(block, axis, k) for k in range(1, SIDE)]


def turned_and_summed(parts, axis):
    sums = parts[0]
    got = [turned(parts[k].astype(jnp.float16), axis, -k) for k in range(1, SIDE)]
    for part in got:
        sums = sums + part.astype(jnp.float32)
    return lax.optimization_barrier(sums)


def digits_kernel(got_ref, row_ref):
    rest = jnp.sum(got_ref[...], axis=0) * (1.0 / TOP)
    lanes = lax.broadcasted_iota(jnp.int32, rest.shape, 1)
    row = jnp.zeros(rest.shape, jnp.float32)
    for k in range(DIGITS):
        rest = rest * BASE
        digit = jnp.floor(rest)
        rest = rest - digit
        row = jnp.where(lanes == k, digit, row)
    row_ref[...] = row


def digit_row(got):
    return pl.pallas_call(
        digits_kernel,
        out_shape=jax.ShapeDtypeStruct(got.shape[1:], jnp.float32),
        in_specs=[VMEM],
        out_specs=VMEM,
        compiler_params=pltpu.CompilerParams(vmem_limit_bytes=4 * 2**20),
    )(got)[:1]


def from_row(row):
    worth = jnp.zeros(row.shape, jnp.float32)
    lanes = jnp.arange(row.shape[0], dtype=jnp.int32)
    for k in range(DIGITS):
        worth = jnp.where(lanes == k, TOP / BASE ** (k + 1), worth)
    return jnp.sum(row * worth)


def sent_and_summed(parts, axis):
    got = lax.all_to_all(parts, axis, 0, 0, tiled=True)
    sums = got[0].astype(jnp.float32)
    for k in range(1, SIDE):
        sums = sums + got[k].astype(jnp.float32)
    return sums


def block_mask(tile_mask):
    x, zb, za, c, y = (lax.axis_index(n) for n in ("x", "zb", "za", "c", "y"))
    tiles = tile_mask.shape[0]

    def tile_of(xs, zbs, zas, cs, ys):
        return (((xs * 2 + zbs) * 4 + zas) * 2 + cs) * 2 + ys // 2

    k = jnp.arange(16, dtype=jnp.int32)
    image_tiles = tile_of((x - k // 4) % 4, zb, (za - k % 4) % 4, c, y)
    k = jnp.arange(32, dtype=jnp.int32)
    text_cores = jnp.where(k < 16, c, 1 - c)
    text_tiles = tile_of(x, k % 2, za, text_cores, (k // 4) % 4)
    every = jnp.arange(tiles, dtype=jnp.int32)
    left = (text_tiles[:, None] == every[None]).astype(jnp.float32)
    right = (image_tiles[:, None] == every[None]).astype(jnp.float32)
    chosen = lax.dot_general(right, tile_mask.astype(jnp.float32), (((1,), (0,)), ((), ())))
    return lax.dot_general(left, chosen, (((1,), (1,)), ((), ())))


def mask_rows(tile_mask, rows):
    i = jnp.arange(16 * rows, dtype=jnp.int32)
    right = (jnp.arange(16)[:, None] == i[None] // rows).astype(jnp.float32)
    return jnp.dot(block_mask(tile_mask), right)


def back(values, inverse, grads):
    unit = values * inverse
    return inverse * (grads - unit * jnp.sum(unit * grads, axis=-1, keepdims=True))


def step(images, texts, tile_mask):
    rows, width = images.shape
    slots, image_bf = normalized(texts, images)
    got = lax.all_to_all(slots, ZB, 0, 0, tiled=True)
    images = images.astype(jnp.float32)
    texts = texts.astype(jnp.float32)
    image_inverse = inverse_norm(images)
    text_inverse = inverse_norm(texts)
    near = all_turned(image_bf, "za")
    near = jnp.concatenate(near, axis=0)
    parts = all_turned(near, "x")
    sent = jnp.broadcast_to(got.reshape(1, SIDE * rows, width), (SIDE, SIDE * rows, width))
    own_texts = lax.all_to_all(sent, "y", 0, 0, tiled=True).reshape(16 * rows, width)
    other_texts = swapped(own_texts)
    masked = mask_rows(tile_mask, rows)
    own_text = (lax.axis_index("y") * SIDE + lax.axis_index(ZB)).reshape(1, 1)
    peers = lax.axis_size(IMAGE_GROUP)
    coef, loss, group = pair_terms(
        own_text, masked, parts, own_texts, other_texts, peers
    )
    loss = lax.all_to_all(loss, IMAGE_GROUP, 0, 0, tiled=True)
    other_sums = jnp.dot(coef[16 * rows :], group, preferred_element_type=jnp.float32)
    other_sums = swapped(other_sums)
    image_parts = lax.dot_general(
        coef[: 16 * rows], own_texts, (((0,), (0,)), ((), ())), preferred_element_type=jnp.float32
    ) + lax.dot_general(
        coef[16 * rows :], other_texts, (((0,), (0,)), ((), ())), preferred_element_type=jnp.float32
    )
    own_sums = jnp.dot(coef[: 16 * rows], group, preferred_element_type=jnp.float32)
    payload = lax.optimization_barrier((own_sums + other_sums).astype(jnp.float16))
    row = digit_row(loss)
    lanes = lax.broadcasted_iota(jnp.int32, (1, width + SPARE), 1)
    row = jnp.pad(row, ((0, 0), (width, 0))).astype(jnp.float16)
    payload = jnp.where(lanes >= width, row, jnp.pad(payload, ((0, 0), (0, SPARE))))
    text_parts = sent_and_summed(payload.reshape(SIDE, SIDE * rows, -1), "y")
    image_parts = turned_and_summed(image_parts.reshape(SIDE, SIDE * rows, width), "x")
    text_parts = text_parts.astype(jnp.float16).reshape(SIDE, rows, -1)
    text_sums = sent_and_summed(text_parts, ZB)
    image_sums = turned_and_summed(image_parts.reshape(SIDE, rows, width), "za")
    loss = from_row(text_sums[0, width:])

    zero = tile_mask == 0
    size = tile_mask.shape[0]
    diagonal = jnp.eye(size, dtype=jnp.bool_)
    pairs = jnp.sum(jnp.where(zero, TILE * TILE, jnp.where(diagonal, TILE, 0)))
    return (
        back(images, image_inverse, TEMP * image_sums),
        back(texts, text_inverse, TEMP * text_sums[:, :width]),
        loss / pairs.astype(jnp.float32),
    )


def solution(mesh):
    finer = Mesh(mesh.devices.reshape(4, 2, 4, 2, 4, 2), ("y", "zh", "x", "zb", "za", "c"))
    placed = P(ROWS_AXES, None)
    return jax.shard_map(
        step,
        mesh=finer,
        in_specs=(placed, placed, P()),
        out_specs=(placed, placed, P()),
        check_vma=False,
    )
```

```python
import jax
import jax.numpy as jnp
from jax import lax
from jax.experimental import pallas as pl
from jax.experimental.pallas import tpu as pltpu
from jax.sharding import Mesh
from jax.sharding import PartitionSpec as P


TILE = 128
TEMP = 10.0
BIAS = -2.0
EPS = 1e-06
ROWS_AXES = ("x", "zb", "za", "c", "y", "zh")
ZB = ("zh", "zb")
IMAGE_GROUP = ("x", "za", "c")
SIDE = 4
DIGITS = 7
BASE = 512.0
TOP = 2.0**32
SPARE = 128
CHUNK = 256

VMEM = pl.BlockSpec(memory_space=pltpu.VMEM)
HBM = pl.BlockSpec(memory_space=pltpu.HBM)


def inverse_norm(values):
    return lax.rsqrt(jnp.sum(values * values, axis=-1, keepdims=True) + EPS)


def held(value):
    return pltpu.with_memory_space_constraint(value, pltpu.HBM)


def slots_kernel(texts_hbm_ref, images_hbm_ref, slots_ref, images_ref, fetched_ref, arrived):
    copies = [
        pltpu.make_async_copy(source, fetched_ref.at[k], arrived.at[k])
        for k, source in enumerate((texts_hbm_ref, images_hbm_ref))
    ]
    for copy in copies:
        copy.start()
    units = []
    for k, copy in enumerate(copies):
        copy.wait()
        values = fetched_ref[k].astype(jnp.float32)
        units.append((values * inverse_norm(values)).astype(jnp.bfloat16))
    for k in range(SIDE):
        slots_ref[k] = units[0]
    images_ref[...] = units[1]


def normalized(texts, images):
    return pl.pallas_call(
        slots_kernel,
        out_shape=(
            jax.ShapeDtypeStruct((SIDE, *texts.shape), jnp.bfloat16),
            jax.ShapeDtypeStruct(images.shape, jnp.bfloat16),
        ),
        in_specs=[HBM] * 2,
        out_specs=(VMEM,) * 2,
        scratch_shapes=[
            pltpu.VMEM((2, *texts.shape), jnp.bfloat16),
            pltpu.SemaphoreType.DMA((2,)),
        ],
        compiler_params=pltpu.CompilerParams(vmem_limit_bytes=4 * 2**20),
    )(held(texts), held(images))


def pair_kernel(own_text_ref, masked_ref, group_ref, own_ref, other_ref, coef_ref, loss_ref):
    group = group_ref[...]
    images, _ = group.shape
    half = own_ref.shape[0]
    rows = 2 * half // masked_ref.shape[0]
    shape = (CHUNK, images)
    columns = lax.broadcasted_iota(jnp.int32, shape, 1)
    diagonal = columns - lax.broadcasted_iota(jnp.int32, shape, 0)
    loss = jnp.zeros((8, images), jnp.float32)
    for texts_ref, base in ((other_ref, half), (own_ref, 0)):
        for at in range(0, half, CHUNK):
            logits = TEMP * lax.dot_general(
                texts_ref[at : at + CHUNK],
                group,
                (((1,), (1,)), ((), ())),
                preferred_element_type=jnp.float32,
            )
            logits = logits + BIAS
            first = (base + at) // rows
            masked = masked_ref[first : first + CHUNK // rows]
            masked = jnp.broadcast_to(masked[:, None], (CHUNK // rows, rows, images)).reshape(shape)
            valid = masked < 0.5
            small = jnp.exp(-jnp.abs(logits))
            soft = jnp.maximum(logits, 0.0) + jnp.log1p(small)
            sigmoid = jnp.where(logits >= 0.0, 1.0, small) / (1.0 + small)
            if base == 0:
                matched = (diagonal == at - own_text_ref[0, 0] * rows) & (columns < rows)
                soft = soft - jnp.where(matched, logits, 0.0)
                sigmoid = sigmoid - jnp.where(matched, 1.0, 0.0)
                valid = valid | matched
            terms = jnp.where(valid, soft, 0.0)
            loss = loss + jnp.sum(terms.reshape(CHUNK // 8, 8, images), axis=0)
            coef = jnp.where(valid, sigmoid, 0.0).astype(jnp.bfloat16)
            coef_ref[base + at : base + at + CHUNK] = coef
    total = jnp.sum(jnp.sum(loss, axis=0, keepdims=True), axis=1, keepdims=True)
    loss_ref[...] = jnp.broadcast_to(total[None], loss_ref.shape)


def pair_terms(own_text, masked, group, own_texts, other_texts, peers):
    images = group.shape[0]
    half = own_texts.shape[0]
    return pl.pallas_call(
        pair_kernel,
        out_shape=(
            pltpu.HBM((2 * half, images), jnp.bfloat16),
            pltpu.HBM((peers, 8, 128), jnp.float32),
        ),
        in_specs=[pl.BlockSpec(memory_space=pltpu.SMEM)] + [VMEM] * 4,
        out_specs=(VMEM,) * 2,
        compiler_params=pltpu.CompilerParams(vmem_limit_bytes=20 * 2**20),
    )(own_text, masked, group, own_texts, other_texts)


def swapped(value):
    return lax.ppermute(value, "c", [(0, 1), (1, 0)])


def turned(value, axis, steps):
    return lax.ppermute(value, axis, [(k, (k + steps) % SIDE) for k in range(SIDE)])


def all_turned(block, axis, way):
    return [block] + [turned(block, axis, way * k) for k in range(1, SIDE)]


def turned_and_summed(parts, axis, way):
    sums = parts[0]
    got = [turned(parts[k].astype(jnp.float16), axis, -way * k) for k in range(1, SIDE)]
    for part in got:
        sums = sums + part.astype(jnp.float32)
    return lax.optimization_barrier(sums)


def digits_kernel(got_ref, row_ref):
    rest = jnp.sum(got_ref[...], axis=0) * (1.0 / TOP)
    lanes = lax.broadcasted_iota(jnp.int32, rest.shape, 1)
    row = jnp.zeros(rest.shape, jnp.float32)
    for k in range(DIGITS):
        rest = rest * BASE
        digit = jnp.floor(rest)
        rest = rest - digit
        row = jnp.where(lanes == k, digit, row)
    row_ref[...] = row


def digit_row(got):
    return pl.pallas_call(
        digits_kernel,
        out_shape=jax.ShapeDtypeStruct(got.shape[1:], jnp.float32),
        in_specs=[VMEM],
        out_specs=VMEM,
        compiler_params=pltpu.CompilerParams(vmem_limit_bytes=4 * 2**20),
    )(got)[:1]


def from_row(row):
    worth = jnp.zeros(row.shape, jnp.float32)
    lanes = jnp.arange(row.shape[0], dtype=jnp.int32)
    for k in range(DIGITS):
        worth = jnp.where(lanes == k, TOP / BASE ** (k + 1), worth)
    return jnp.sum(row * worth)


def sent_and_summed(parts, axis):
    got = lax.all_to_all(parts, axis, 0, 0, tiled=True)
    sums = got[0].astype(jnp.float32)
    for k in range(1, SIDE):
        sums = sums + got[k].astype(jnp.float32)
    return sums


def block_mask(tile_mask):
    x, zb, za, c, y = (lax.axis_index(n) for n in ("x", "zb", "za", "c", "y"))
    tiles = tile_mask.shape[0]

    def tile_of(xs, zbs, zas, cs, ys):
        return (((xs * 2 + zbs) * 4 + zas) * 2 + cs) * 2 + ys // 2

    k = jnp.arange(16, dtype=jnp.int32)
    image_tiles = tile_of((x + k // 4) % 4, zb, (za - k % 4) % 4, c, y)
    k = jnp.arange(32, dtype=jnp.int32)
    text_cores = jnp.where(k < 16, c, 1 - c)
    text_tiles = tile_of(x, k % 2, za, text_cores, (k // 4) % 4)
    every = jnp.arange(tiles, dtype=jnp.int32)
    left = (text_tiles[:, None] == every[None]).astype(jnp.float32)
    right = (image_tiles[:, None] == every[None]).astype(jnp.float32)
    chosen = lax.dot_general(right, tile_mask.astype(jnp.float32), (((1,), (0,)), ((), ())))
    return lax.dot_general(left, chosen, (((1,), (1,)), ((), ())))


def mask_rows(tile_mask, rows):
    i = jnp.arange(16 * rows, dtype=jnp.int32)
    right = (jnp.arange(16)[:, None] == i[None] // rows).astype(jnp.float32)
    return jnp.dot(block_mask(tile_mask), right)


def back(values, inverse, grads):
    unit = values * inverse
    return inverse * (grads - unit * jnp.sum(unit * grads, axis=-1, keepdims=True))


def step(images, texts, tile_mask):
    rows, width = images.shape
    slots, image_bf = normalized(texts, images)
    got = lax.all_to_all(slots, ZB, 0, 0, tiled=True)
    images = images.astype(jnp.float32)
    texts = texts.astype(jnp.float32)
    image_inverse = inverse_norm(images)
    text_inverse = inverse_norm(texts)
    near = all_turned(image_bf, "za", 1)
    near = jnp.concatenate(near, axis=0)
    parts = all_turned(near, "x", -1)
    sent = jnp.broadcast_to(got.reshape(1, SIDE * rows, width), (SIDE, SIDE * rows, width))
    own_texts = lax.all_to_all(sent, "y", 0, 0, tiled=True).reshape(16 * rows, width)
    other_texts = swapped(own_texts)
    masked = mask_rows(tile_mask, rows)
    own_text = (lax.axis_index("y") * SIDE + lax.axis_index(ZB)).reshape(1, 1)
    peers = lax.axis_size(IMAGE_GROUP)
    group = jnp.concatenate(parts, axis=0)
    coef, loss = pair_terms(own_text, masked, group, own_texts, other_texts, peers)
    loss = lax.all_to_all(loss, IMAGE_GROUP, 0, 0, tiled=True)
    other_sums = jnp.dot(coef[16 * rows :], group, preferred_element_type=jnp.float32)
    other_sums = swapped(other_sums)
    image_parts = lax.dot_general(
        coef[: 16 * rows], own_texts, (((0,), (0,)), ((), ())), preferred_element_type=jnp.float32
    ) + lax.dot_general(
        coef[16 * rows :], other_texts, (((0,), (0,)), ((), ())), preferred_element_type=jnp.float32
    )
    own_sums = jnp.dot(coef[: 16 * rows], group, preferred_element_type=jnp.float32)
    payload = lax.optimization_barrier((own_sums + other_sums).astype(jnp.float16))
    row = digit_row(loss)
    lanes = lax.broadcasted_iota(jnp.int32, (1, width + SPARE), 1)
    row = jnp.pad(row, ((0, 0), (width, 0))).astype(jnp.float16)
    payload = jnp.where(lanes >= width, row, jnp.pad(payload, ((0, 0), (0, SPARE))))
    text_parts = sent_and_summed(payload.reshape(SIDE, SIDE * rows, -1), "y")
    image_parts = turned_and_summed(image_parts.reshape(SIDE, SIDE * rows, width), "x", -1)
    text_parts = text_parts.astype(jnp.float16).reshape(SIDE, rows, -1)
    text_sums = sent_and_summed(text_parts, ZB)
    image_sums = turned_and_summed(image_parts.reshape(SIDE, rows, width), "za", 1)
    loss = from_row(text_sums[0, width:])

    zero = tile_mask == 0
    size = tile_mask.shape[0]
    diagonal = jnp.eye(size, dtype=jnp.bool_)
    pairs = jnp.sum(jnp.where(zero, TILE * TILE, jnp.where(diagonal, TILE, 0)))
    return (
        back(images, image_inverse, TEMP * image_sums),
        back(texts, text_inverse, TEMP * text_sums[:, :width]),
        loss / pairs.astype(jnp.float32),
    )


def solution(mesh):
    finer = Mesh(mesh.devices.reshape(4, 2, 4, 2, 4, 2), ("y", "zh", "x", "zb", "za", "c"))
    placed = P(ROWS_AXES, None)
    return jax.shard_map(
        step,
        mesh=finer,
        in_specs=(placed, placed, P()),
        out_specs=(placed, placed, P()),
        check_vma=False,
    )
```

```python
import jax
import jax.numpy as jnp
from jax import lax
from jax.experimental import pallas as pl
from jax.experimental.pallas import tpu as pltpu
from jax.sharding import Mesh
from jax.sharding import PartitionSpec as P


TILE = 128
TEMP = 10.0
BIAS = -2.0
EPS = 1e-06
ROWS_AXES = ("x", "zb", "za", "c", "y", "zh")
ZB = ("zh", "zb")
IMAGE_GROUP = ("x", "za", "c")
SIDE = 4
DIGITS = 7
BASE = 512.0
TOP = 2.0**32
SPARE = 128
CHUNK = 512

VMEM = pl.BlockSpec(memory_space=pltpu.VMEM)
HBM = pl.BlockSpec(memory_space=pltpu.HBM)


def inverse_norm(values):
    return lax.rsqrt(jnp.sum(values * values, axis=-1, keepdims=True) + EPS)


def held(value):
    return pltpu.with_memory_space_constraint(value, pltpu.HBM)


def slots_kernel(texts_hbm_ref, images_hbm_ref, slots_ref, images_ref, fetched_ref, arrived):
    copies = [
        pltpu.make_async_copy(source, fetched_ref.at[k], arrived.at[k])
        for k, source in enumerate((texts_hbm_ref, images_hbm_ref))
    ]
    for copy in copies:
        copy.start()
    units = []
    for k, copy in enumerate(copies):
        copy.wait()
        values = fetched_ref[k].astype(jnp.float32)
        units.append((values * inverse_norm(values)).astype(jnp.bfloat16))
    for k in range(SIDE):
        slots_ref[k] = units[0]
    images_ref[...] = units[1]


def normalized(texts, images):
    return pl.pallas_call(
        slots_kernel,
        out_shape=(
            jax.ShapeDtypeStruct((SIDE, *texts.shape), jnp.bfloat16),
            jax.ShapeDtypeStruct(images.shape, jnp.bfloat16),
        ),
        in_specs=[HBM] * 2,
        out_specs=(VMEM,) * 2,
        scratch_shapes=[
            pltpu.VMEM((2, *texts.shape), jnp.bfloat16),
            pltpu.SemaphoreType.DMA((2,)),
        ],
        compiler_params=pltpu.CompilerParams(vmem_limit_bytes=4 * 2**20),
    )(held(texts), held(images))


def pair_kernel(own_text_ref, masked_hbm_ref, *refs):
    part_refs, (own_ref, other_ref) = refs[:SIDE], refs[SIDE : SIDE + 2]
    coef_ref, loss_ref, group_ref, masked_ref, arrived = refs[SIDE + 2 :]
    near = part_refs[0].shape[0]
    copies = [
        pltpu.make_async_copy(part_refs[k], group_ref.at[pl.ds(k * near, near)], arrived.at[k])
        for k in range(SIDE)
    ]
    copies.append(pltpu.make_async_copy(masked_hbm_ref, masked_ref, arrived.at[SIDE]))
    for copy in copies:
        copy.start()
    for copy in copies:
        copy.wait()
    group = group_ref[...]
    images, _ = group.shape
    half = own_ref.shape[0]
    rows = 2 * half // masked_ref.shape[0]
    shape = (CHUNK, images)
    columns = lax.broadcasted_iota(jnp.int32, shape, 1)
    diagonal = columns - lax.broadcasted_iota(jnp.int32, shape, 0)
    loss = jnp.zeros((8, images), jnp.float32)
    for texts_ref, base in ((other_ref, half), (own_ref, 0)):
        for at in range(0, half, CHUNK):
            logits = TEMP * lax.dot_general(
                texts_ref[at : at + CHUNK],
                group,
                (((1,), (1,)), ((), ())),
                preferred_element_type=jnp.float32,
            )
            logits = logits + BIAS
            first = (base + at) // rows
            masked = masked_ref[first : first + CHUNK // rows]
            masked = jnp.broadcast_to(masked[:, None], (CHUNK // rows, rows, images)).reshape(shape)
            valid = masked < 0.5
            small = jnp.exp(-jnp.abs(logits))
            soft = jnp.maximum(logits, 0.0) + jnp.log1p(small)
            sigmoid = jnp.where(logits >= 0.0, 1.0, small) / (1.0 + small)
            if base == 0:
                matched = (diagonal == at - own_text_ref[0, 0] * rows) & (columns < rows)
                soft = soft - jnp.where(matched, logits, 0.0)
                sigmoid = sigmoid - jnp.where(matched, 1.0, 0.0)
                valid = valid | matched
            terms = jnp.where(valid, soft, 0.0)
            loss = loss + jnp.sum(terms.reshape(CHUNK // 8, 8, images), axis=0)
            coef = jnp.where(valid, sigmoid, 0.0).astype(jnp.bfloat16)
            coef_ref[base + at : base + at + CHUNK] = coef
    total = jnp.sum(jnp.sum(loss, axis=0, keepdims=True), axis=1, keepdims=True)
    loss_ref[...] = jnp.broadcast_to(total[None], loss_ref.shape)


def pair_terms(own_text, masked, parts, own_texts, other_texts, peers):
    near, width = parts[0].shape
    half = own_texts.shape[0]
    images = SIDE * near
    return pl.pallas_call(
        pair_kernel,
        out_shape=(
            pltpu.HBM((2 * half, images), jnp.bfloat16),
            pltpu.HBM((peers, 8, 128), jnp.float32),
            jax.ShapeDtypeStruct((images, width), jnp.bfloat16),
        ),
        in_specs=[pl.BlockSpec(memory_space=pltpu.SMEM)] + [HBM] * (SIDE + 1) + [VMEM] * 2,
        out_specs=(VMEM,) * 3,
        scratch_shapes=[
            pltpu.VMEM(masked.shape, jnp.float32),
            pltpu.SemaphoreType.DMA((SIDE + 1,)),
        ],
        compiler_params=pltpu.CompilerParams(vmem_limit_bytes=20 * 2**20),
    )(own_text, *(held(a) for a in (masked, *parts)), own_texts, other_texts)


def swapped(value):
    return lax.ppermute(value, "c", [(0, 1), (1, 0)])


def turned(value, axis, steps):
    return lax.ppermute(value, axis, [(k, (k + steps) % SIDE) for k in range(SIDE)])


def all_turned(block, axis, way):
    return [block] + [turned(block, axis, way * k) for k in range(1, SIDE)]


def turned_and_summed(parts, axis, way):
    sums = parts[0]
    got = [turned(parts[k].astype(jnp.float16), axis, -way * k) for k in range(1, SIDE)]
    for part in got:
        sums = sums + part.astype(jnp.float32)
    return lax.optimization_barrier(sums)


def digits_kernel(got_ref, row_ref):
    rest = jnp.sum(got_ref[...], axis=0) * (1.0 / TOP)
    lanes = lax.broadcasted_iota(jnp.int32, rest.shape, 1)
    row = jnp.zeros(rest.shape, jnp.float32)
    for k in range(DIGITS):
        rest = rest * BASE
        digit = jnp.floor(rest)
        rest = rest - digit
        row = jnp.where(lanes == k, digit, row)
    row_ref[...] = row


def digit_row(got):
    return pl.pallas_call(
        digits_kernel,
        out_shape=jax.ShapeDtypeStruct(got.shape[1:], jnp.float32),
        in_specs=[VMEM],
        out_specs=VMEM,
        compiler_params=pltpu.CompilerParams(vmem_limit_bytes=4 * 2**20),
    )(got)[:1]


def from_row(row):
    worth = jnp.zeros(row.shape, jnp.float32)
    lanes = jnp.arange(row.shape[0], dtype=jnp.int32)
    for k in range(DIGITS):
        worth = jnp.where(lanes == k, TOP / BASE ** (k + 1), worth)
    return jnp.sum(row * worth)


def sent_and_summed(parts, axis):
    got = lax.all_to_all(parts, axis, 0, 0, tiled=True)
    sums = got[0].astype(jnp.float32)
    for k in range(1, SIDE):
        sums = sums + got[k].astype(jnp.float32)
    return sums


def block_mask(tile_mask):
    x, zb, za, c, y = (lax.axis_index(n) for n in ("x", "zb", "za", "c", "y"))
    tiles = tile_mask.shape[0]

    def tile_of(xs, zbs, zas, cs, ys):
        return (((xs * 2 + zbs) * 4 + zas) * 2 + cs) * 2 + ys // 2

    k = jnp.arange(16, dtype=jnp.int32)
    image_tiles = tile_of((x + k // 4) % 4, zb, (za - k % 4) % 4, c, y)
    k = jnp.arange(32, dtype=jnp.int32)
    text_cores = jnp.where(k < 16, c, 1 - c)
    text_tiles = tile_of(x, k % 2, za, text_cores, (k // 4) % 4)
    every = jnp.arange(tiles, dtype=jnp.int32)
    left = (text_tiles[:, None] == every[None]).astype(jnp.float32)
    right = (image_tiles[:, None] == every[None]).astype(jnp.float32)
    chosen = lax.dot_general(right, tile_mask.astype(jnp.float32), (((1,), (0,)), ((), ())))
    return lax.dot_general(left, chosen, (((1,), (1,)), ((), ())))


def mask_rows(tile_mask, rows):
    i = jnp.arange(16 * rows, dtype=jnp.int32)
    right = (jnp.arange(16)[:, None] == i[None] // rows).astype(jnp.float32)
    return jnp.dot(block_mask(tile_mask), right)


def back(values, inverse, grads):
    unit = values * inverse
    return inverse * (grads - unit * jnp.sum(unit * grads, axis=-1, keepdims=True))


def step(images, texts, tile_mask):
    rows, width = images.shape
    slots, image_bf = normalized(texts, images)
    got = lax.all_to_all(slots, ZB, 0, 0, tiled=True)
    images = images.astype(jnp.float32)
    texts = texts.astype(jnp.float32)
    image_inverse = inverse_norm(images)
    text_inverse = inverse_norm(texts)
    near = all_turned(image_bf, "za", 1)
    near = jnp.concatenate(near, axis=0)
    parts = all_turned(near, "x", -1)
    sent = jnp.broadcast_to(got.reshape(1, SIDE * rows, width), (SIDE, SIDE * rows, width))
    own_texts = lax.all_to_all(sent, "y", 0, 0, tiled=True).reshape(16 * rows, width)
    other_texts = swapped(own_texts)
    masked = mask_rows(tile_mask, rows)
    own_text = (lax.axis_index("y") * SIDE + lax.axis_index(ZB)).reshape(1, 1)
    peers = lax.axis_size(IMAGE_GROUP)
    coef, loss, group = pair_terms(
        own_text, masked, parts, own_texts, other_texts, peers
    )
    loss = lax.all_to_all(loss, IMAGE_GROUP, 0, 0, tiled=True)
    other_sums = jnp.dot(coef[16 * rows :], group, preferred_element_type=jnp.float32)
    other_sums = swapped(other_sums)
    image_parts = lax.dot_general(
        coef[: 16 * rows], own_texts, (((0,), (0,)), ((), ())), preferred_element_type=jnp.float32
    ) + lax.dot_general(
        coef[16 * rows :], other_texts, (((0,), (0,)), ((), ())), preferred_element_type=jnp.float32
    )
    own_sums = jnp.dot(coef[: 16 * rows], group, preferred_element_type=jnp.float32)
    payload = lax.optimization_barrier((own_sums + other_sums).astype(jnp.float16))
    row = digit_row(loss)
    lanes = lax.broadcasted_iota(jnp.int32, (1, width + SPARE), 1)
    row = jnp.pad(row, ((0, 0), (width, 0))).astype(jnp.float16)
    payload = jnp.where(lanes >= width, row, jnp.pad(payload, ((0, 0), (0, SPARE))))
    text_parts = sent_and_summed(payload.reshape(SIDE, SIDE * rows, -1), "y")
    image_parts = turned_and_summed(image_parts.reshape(SIDE, SIDE * rows, width), "x", -1)
    text_parts = text_parts.astype(jnp.float16).reshape(SIDE, rows, -1)
    text_sums = sent_and_summed(text_parts, ZB)
    image_sums = turned_and_summed(image_parts.reshape(SIDE, rows, width), "za", 1)
    loss = from_row(text_sums[0, width:])

    zero = tile_mask == 0
    size = tile_mask.shape[0]
    diagonal = jnp.eye(size, dtype=jnp.bool_)
    pairs = jnp.sum(jnp.where(zero, TILE * TILE, jnp.where(diagonal, TILE, 0)))
    return (
        back(images, image_inverse, TEMP * image_sums),
        back(texts, text_inverse, TEMP * text_sums[:, :width]),
        loss / pairs.astype(jnp.float32),
    )


def solution(mesh):
    finer = Mesh(mesh.devices.reshape(4, 2, 4, 2, 4, 2), ("y", "zh", "x", "zb", "za", "c"))
    placed = P(ROWS_AXES, None)
    return jax.shard_map(
        step,
        mesh=finer,
        in_specs=(placed, placed, P()),
        out_specs=(placed, placed, P()),
        check_vma=False,
    )
```
